512 devices in a mesh: dp: 16 (over y, x), expert: 32 (over z, core).
Axes of the slice: x: 4, y: 4, z: 16, core: 2. Of those that a mesh axis runs over, the one named last changes fastest.
Arguments:
- query_rows: bfloat16 [32, 2048, 2048], P('dp', 'expert'), may hold values from -4 to 4
- key_rows: bfloat16 [32, 2048, 256], P('dp', 'expert'), may hold values from -4 to 4
- value_rows: bfloat16 [32, 2048, 256], P('dp', 'expert'), may hold values from -6 to 6
- gate_logits: bfloat16 [32, 2048, 2048], P('dp', 'expert'), may hold values from -6 to 6
- gated_grad: bfloat16 [32, 2048, 2048], P('dp', 'expert'), may hold values from -6 to 6
- moe_input: bfloat16 [65536, 2048], P(('dp', 'expert')), may hold values from -6 to 6
- out_grad: bfloat16 [65536, 2048], P(('dp', 'expert')), may hold values from -24 to 24
- routes: int32 [65536, 10], P(('dp', 'expert')), may hold values from 0 to 511, as said below
- route_weights: bfloat16 [65536, 10], P(('dp', 'expert')), may hold values from 0.019897461 to 0.29882812
- gate_proj: bfloat16 [32, 2048, 256], P('expert', 'dp'), may hold values from -0.125 to 0.125
- up_proj: bfloat16 [32, 2048, 256], P('expert', 'dp'), may hold values from -0.125 to 0.125
- down_proj: bfloat16 [32, 256, 2048], P('expert', None, 'dp'), may hold values from -0.375 to 0.375
Outputs:
- query_grad: bfloat16 [32, 2048, 2048], P('dp', 'expert')
- key_grad: bfloat16 [32, 2048, 256], P('dp', 'expert')
- value_grad: bfloat16 [32, 2048, 256], P('dp', 'expert')
- gate_grad: bfloat16 [32, 2048, 2048], P('dp', 'expert')
- input_grad: bfloat16 [65536, 2048], P(('dp', 'expert'))
- route_grad: bfloat16 [65536, 10], P(('dp', 'expert'))
- gate_proj_grad: float32 [32, 2048, 256], P('expert', 'dp')
- up_proj_grad: float32 [32, 2048, 256], P('expert', 'dp')
- down_proj_grad: float32 [32, 256, 2048], P('expert', None, 'dp')
The draws below stay inside these ranges and needn't reach their ends.
Inputs may be any that keep to these rules, and one draw needn't show every extreme that they name: `routes`: each token names 10 different experts. A token names at most one expert below 32; the 128 tokens of one block name each such expert at most 2 times, and in every data group one expert below 32 is named exactly 2 times by every block of the group.
All inputs are finite; a program needn't handle non-finite values.
Results may differ from the reference program's by a relative error of at most 0.035.
Values may be sent and summed in bfloat16 or wider, within the bound.
A program may use at most 64 MiB of HBM per device.

```python
import jax
import jax.numpy as jnp
from jax import lax

D = 2048
HEADS = 8
HEAD = 256
EXP_HID = 256
EXPERTS = 512
TOP = 10
CAP = 2
TOK_DEV = 128
SHARD = 64
LEN = 2048
BATCH = 32
TOKENS = 65536
FLIGHT = 32
N_DP = 16
N_EXPERT = 32


def draw_query_rows(key, part):
    own_key = jax.random.fold_in(key, 11)
    values = jnp.clip(jax.random.normal(own_key, (BATCH, LEN, HEADS, HEAD), jnp.float32), -4.0, 4.0)
    return values.reshape(BATCH, LEN, HEADS * HEAD).astype(jnp.bfloat16)


def draw_key_rows(key, part):
    own_key = jax.random.fold_in(key, 21)
    values = jnp.clip(jax.random.normal(own_key, (BATCH, LEN, HEAD), jnp.float32), -4.0, 4.0)
    return values.astype(jnp.bfloat16)


def route_block(key, block_index):
    flight = N_EXPERT
    group_index = block_index // N_EXPERT
    hot_expert = jax.random.randint(jax.random.fold_in(key, 50000 + group_index), (), 0, flight)
    block_key = jax.random.fold_in(key, block_index)
    counts = jax.random.randint(jax.random.fold_in(block_key, 1), (flight,), 0, CAP + 1)
    counts = jnp.where(jnp.arange(flight) == hot_expert, CAP, counts)
    token_order = jax.random.permutation(jax.random.fold_in(block_key, 2), TOK_DEV)
    slot_index = jnp.arange(flight * CAP)
    expert_of = slot_index // CAP
    slot_used = slot_index % CAP < counts[expert_of]
    live_expert = jnp.full((TOK_DEV,), -1, jnp.int32).at[token_order[:flight * CAP]].set(jnp.where(slot_used, expert_of, -1).astype(jnp.int32))
    column = jax.random.randint(jax.random.fold_in(block_key, 3), (TOK_DEV,), 0, TOP)
    offset_base = jax.random.randint(jax.random.fold_in(block_key, 4), (TOK_DEV,), 0, EXPERTS - flight)
    others = flight + (offset_base[:, None] + jnp.arange(TOP)[None, :]) % (EXPERTS - flight)
    placed = (jnp.arange(TOP)[None, :] == column[:, None]) & (live_expert[:, None] >= 0)
    return jnp.where(placed, live_expert[:, None], others).astype(jnp.int32)


def draw_routes(key, part):
    block_ids = jnp.arange(N_DP * N_EXPERT)
    routed = jax.vmap(partial_block(key))(block_ids)
    return routed.reshape(TOKENS, TOP)


def partial_block(key):

    def make_block(block_index):
        return route_block(key, block_index)
    return make_block


def block_levels(key, dims, split, smallest, largest):
    factor_of, own = 1.0, jax.random.fold_in(key, 6)
    for axis_at, blocks in split:
        draws = jnp.exp(jax.random.uniform(jax.random.fold_in(own, axis_at), (blocks,), jnp.float32, smallest / len(split), largest / len(split)))
        factor_of = factor_of * jnp.repeat(draws, dims[axis_at] // blocks).reshape([-1 if axis == axis_at else 1 for axis in range(len(dims))])
    return factor_of


def noise(key, extent, spread, bound, pieces=(), held_as=jnp.bfloat16):
    level = block_levels(key, extent, pieces, -0.22, 0.18) if pieces else 1.0
    array = jax.random.normal(key, extent, jnp.float32) * spread * level
    return jnp.minimum(jnp.maximum(array, -bound), bound).astype(held_as)


def setup_inputs(seed: int = 0) -> dict:
    key_of = jax.random.split(jax.random.key(seed), 13)
    return {
        "query_rows": draw_query_rows(jax.random.fold_in(key_of[12], 71), 0),
        "key_rows": draw_key_rows(jax.random.fold_in(key_of[12], 71), 0),
        "value_rows": noise(key_of[2], (BATCH, LEN, HEAD), 1.0, 6.0, ((0, 16), (1, 32))),
        "gate_logits": noise(key_of[3], (BATCH, LEN, HEADS * HEAD), 1.0, 6.0, ((0, 16), (1, 32))),
        "gated_grad": noise(key_of[4], (BATCH, LEN, HEADS * HEAD), 1.0, 6.0, ((0, 16), (1, 32))),
        "moe_input": noise(key_of[5], (TOKENS, D), 1.0, 6.0, ((0, 512),)),
        "out_grad": noise(key_of[6], (TOKENS, D), 4.0, 24.0, ((0, 512),)),
        "routes": draw_routes(jax.random.fold_in(key_of[12], 71), 0),
        "route_weights": jnp.clip(0.019897461 + 0.27893066 * jax.random.uniform(key_of[8], (TOKENS, TOP), jnp.float32) ** block_levels(key_of[8], (TOKENS, TOP), ((0, 512),), -0.2, 0.2), 0.019897461, 0.29882812).astype(jnp.bfloat16),
        "gate_proj": noise(key_of[9], (FLIGHT, D, EXP_HID), D ** -0.5, 0.125, ((0, 32), (1, 16))),
        "up_proj": noise(key_of[10], (FLIGHT, D, EXP_HID), D ** -0.5, 0.125, ((0, 32), (1, 16))),
        "down_proj": noise(key_of[11], (FLIGHT, EXP_HID, D), EXP_HID ** -0.5, 0.375, ((0, 32), (2, 16))),
    }


def attend_sequence(operands):
    query_seq, key_seq, value_seq, logit_seq, gated_seq = operands
    score_scale = HEAD ** -0.5
    queries = query_seq.reshape(LEN, HEADS, HEAD).astype(jnp.float32)
    key_wide = key_seq.astype(jnp.float32)
    value_wide = value_seq.astype(jnp.float32)
    scores = jnp.einsum("phd,rd->hpr", queries, key_wide) * score_scale
    causal = (jnp.arange(LEN)[:, None] >= jnp.arange(LEN)[None, :])[None]
    masked = jnp.where(causal, scores, -jnp.inf)
    row_max = jnp.max(masked, axis=2, keepdims=True)
    log_total = row_max + jnp.log(jnp.sum(jnp.exp(masked - row_max), axis=2, keepdims=True))
    exact_probs = jnp.where(causal, jnp.exp(scores - log_total), 0.0)
    probs_low = exact_probs.astype(jnp.bfloat16)
    context = jnp.einsum("hpr,rd->phd", probs_low.astype(jnp.float32), value_wide)
    sigmoid_gate = jax.nn.sigmoid(logit_seq.astype(jnp.float32)).reshape(LEN, HEADS, HEAD)
    upstream = gated_seq.astype(jnp.float32).reshape(LEN, HEADS, HEAD)
    context_grad = (upstream * sigmoid_gate).astype(jnp.bfloat16)
    gate_grad = (upstream * context * sigmoid_gate * (1.0 - sigmoid_gate)).astype(jnp.bfloat16)
    grad_wide = context_grad.astype(jnp.float32)
    grad_dot = jnp.transpose(jnp.sum(grad_wide * context, axis=2))
    prob_grad = jnp.einsum("phd,rd->hpr", grad_wide, value_wide)
    score_grad = (exact_probs * (prob_grad - grad_dot[:, :, None]) * score_scale).astype(jnp.bfloat16)
    score_wide = score_grad.astype(jnp.float32)
    query_grad = jnp.einsum("hpr,rd->phd", score_wide, key_wide).astype(jnp.bfloat16)
    blocked_scores = score_wide.reshape(HEADS, N_EXPERT, SHARD, LEN)
    blocked_probs = probs_low.astype(jnp.float32).reshape(HEADS, N_EXPERT, SHARD, LEN)
    key_parts = jnp.einsum("hnpr,nphd->nrd", blocked_scores, queries.reshape(N_EXPERT, SHARD, HEADS, HEAD)).astype(jnp.bfloat16)
    value_parts = jnp.einsum("hnpr,nphd->nrd", blocked_probs, grad_wide.reshape(N_EXPERT, SHARD, HEADS, HEAD)).astype(jnp.bfloat16)
    key_grad = jnp.sum(key_parts.astype(jnp.float32), axis=0).astype(jnp.bfloat16)
    value_grad = jnp.sum(value_parts.astype(jnp.float32), axis=0).astype(jnp.bfloat16)
    return (query_grad.reshape(LEN, HEADS * HEAD), key_grad, value_grad, gate_grad.reshape(LEN, HEADS * HEAD))


def group_sum(left, right, groups):
    left_wide = left.reshape(groups, -1, left.shape[-1]).astype(jnp.float32)
    right_wide = right.reshape(groups, -1, right.shape[-1]).astype(jnp.float32)
    partial_sums = jnp.einsum("grc,gre->gce", left_wide, right_wide).astype(jnp.bfloat16)
    return jnp.sum(partial_sums.astype(jnp.float32), axis=0)


def expert_pass(operands):
    rows_in, grads_in, weights_in, gate_mat, up_mat, down_mat = operands
    groups = rows_in.shape[0]
    flat_rows = rows_in.reshape(-1, D)
    flat_grads = grads_in.reshape(-1, D)
    gate_pre = jnp.dot(flat_rows, gate_mat, preferred_element_type=jnp.float32)
    up_pre = jnp.dot(flat_rows, up_mat, preferred_element_type=jnp.float32)
    sigmoid_pre = jax.nn.sigmoid(gate_pre)
    silu_value = gate_pre * sigmoid_pre
    hidden = (silu_value * up_pre).astype(jnp.bfloat16)
    expert_out = jnp.dot(hidden, down_mat, preferred_element_type=jnp.float32)
    weight_back = jnp.sum(expert_out * flat_grads.astype(jnp.float32), axis=1).astype(jnp.bfloat16)
    scaled_grad = (weights_in.reshape(-1)[:, None].astype(jnp.float32) * flat_grads.astype(jnp.float32)).astype(jnp.bfloat16)
    hidden_grad = jnp.dot(scaled_grad, down_mat.T, preferred_element_type=jnp.float32)
    slope = sigmoid_pre * (1.0 + gate_pre * (1.0 - sigmoid_pre))
    gate_rows = (hidden_grad * up_pre * slope).astype(jnp.bfloat16)
    up_rows = (hidden_grad * silu_value).astype(jnp.bfloat16)
    input_rows = (jnp.dot(gate_rows, gate_mat.T, preferred_element_type=jnp.float32)
                  + jnp.dot(up_rows, up_mat.T, preferred_element_type=jnp.float32)).astype(jnp.bfloat16)
    gate_total = group_sum(flat_rows, gate_rows, groups)
    up_total = group_sum(flat_rows, up_rows, groups)
    down_total = group_sum(hidden, scaled_grad, groups)
    return input_rows, weight_back, gate_total, up_total, down_total


def reference(query_rows, key_rows, value_rows, gate_logits, gated_grad, moe_input, out_grad, routes, route_weights, gate_proj, up_proj, down_proj):
    query_grad, key_grad, value_grad, gate_grad = lax.map(attend_sequence, (query_rows, key_rows, value_rows, gate_logits, gated_grad))
    blocks = N_DP * N_EXPERT
    slot_total = N_EXPERT * CAP
    route_ids = routes.reshape(blocks, TOK_DEV, TOP)
    live_slot = route_ids < N_EXPERT
    has_live = jnp.any(live_slot, axis=2)
    live_expert = jnp.sum(jnp.where(live_slot, route_ids, 0), axis=2).astype(jnp.int32)
    member = (live_expert[:, :, None] == jnp.arange(N_EXPERT, dtype=jnp.int32)[None, None, :]) & has_live[:, :, None]
    member_count = member.astype(jnp.int32)
    before = jnp.cumsum(member_count, axis=1) - member_count
    slot_rank = jnp.sum(jnp.where(member, before, 0), axis=2).astype(jnp.int32)
    slot_of = jnp.where(has_live, live_expert * CAP + slot_rank, slot_total).astype(jnp.int32)
    token_ids = jnp.broadcast_to(jnp.arange(TOK_DEV, dtype=jnp.int32)[None, :], (blocks, TOK_DEV))
    block_ids = jnp.broadcast_to(jnp.arange(blocks, dtype=jnp.int32)[:, None], (blocks, TOK_DEV))
    table = jnp.full((blocks, slot_total), TOK_DEV, jnp.int32).at[block_ids, slot_of].set(token_ids, mode="drop")
    token_weight = jnp.sum(jnp.where(live_slot, route_weights.reshape(blocks, TOK_DEV, TOP).astype(jnp.float32), 0.0), axis=2).astype(jnp.bfloat16)

    def pick_rows(values):
        padded = jnp.concatenate([values, jnp.zeros((blocks, 1, values.shape[2]), values.dtype)], axis=1)
        return jnp.take_along_axis(padded, table[:, :, None], axis=1)

    def by_expert(values):
        shaped = values.reshape((N_DP, N_EXPERT, N_EXPERT, CAP) + values.shape[2:])
        moved = jnp.moveaxis(shaped, 2, 0)
        return moved.reshape((N_EXPERT, N_DP, N_EXPERT * CAP) + values.shape[2:])

    def back_to_blocks(values):
        shaped = values.reshape((N_EXPERT, N_DP, N_EXPERT, CAP) + values.shape[2:])
        moved = jnp.moveaxis(shaped, 0, 2)
        return moved.reshape((blocks, slot_total) + values.shape[2:])

    rows_all = pick_rows(moe_input.reshape(blocks, TOK_DEV, D))
    grads_all = pick_rows(out_grad.reshape(blocks, TOK_DEV, D))
    weights_all = pick_rows(token_weight[:, :, None])[:, :, 0]
    input_rows, weight_back, gate_total, up_total, down_total = lax.map(
        expert_pass, (by_expert(rows_all), by_expert(grads_all), by_expert(weights_all), gate_proj, up_proj, down_proj))
    input_blocks = back_to_blocks(input_rows.reshape(N_EXPERT, N_DP * N_EXPERT * CAP, D))
    weight_blocks = back_to_blocks(weight_back.reshape(N_EXPERT, N_DP * N_EXPERT * CAP))
    input_padded = jnp.concatenate([input_blocks, jnp.zeros((blocks, 1, D), jnp.bfloat16)], axis=1)
    input_grad = jnp.take_along_axis(input_padded, slot_of[:, :, None], axis=1).reshape(TOKENS, D)
    weight_padded = jnp.concatenate([weight_blocks, jnp.zeros((blocks, 1), jnp.bfloat16)], axis=1)
    token_back = jnp.take_along_axis(weight_padded, slot_of, axis=1)
    route_grad = jnp.where(live_slot, token_back[:, :, None], jnp.zeros((), jnp.bfloat16)).astype(jnp.bfloat16).reshape(TOKENS, TOP)
    return (query_grad, key_grad, value_grad, gate_grad, input_grad, route_grad, gate_total, up_total, down_total)
```

```python
import jax
import jax.numpy as jnp
from jax import lax
from jax.sharding import PartitionSpec as P

HEADS = 8
HEAD = 256
CAP = 2


def keep_state(run_state):
    return run_state


def block_scores(queries, keys_block, block_start, first_position, score_scale):
    scores = (
        jnp.einsum("sphd,srd->shpr", queries, keys_block, preferred_element_type=jnp.float32)
        * score_scale
    )
    query_pos = first_position + jnp.arange(queries.shape[1])
    key_pos = block_start + jnp.arange(keys_block.shape[1])
    allowed = key_pos[None, :] <= query_pos[:, None]
    return (scores, allowed[None, None])


def shards(
    query_rows,
    key_rows,
    value_rows,
    gate_logits,
    gated_grad,
    moe_input,
    out_grad,
    routes,
    route_weights,
    gate_proj,
    up_proj,
    down_proj,
):
    seq_count, shard_len, row_width = query_rows.shape
    devices = lax.axis_size("expert")
    position = lax.axis_index("expert")
    first_position = position * shard_len
    last_position = first_position + shard_len - 1
    total_len = shard_len * devices
    block_len = min(total_len, max(shard_len, 128))
    block_count = total_len // block_len
    shards_per_block = block_len // shard_len
    score_scale = HEAD ** (-0.5)
    queries = query_rows.reshape(seq_count, shard_len, HEADS, HEAD)
    packed = jnp.concatenate([key_rows, value_rows], axis=2)
    gathered = lax.all_gather(packed, "expert", axis=1, tiled=True)

    def take_block(block_index):
        block_start = block_index * block_len
        key_piece = lax.dynamic_slice_in_dim(gathered, block_start, block_len, 1)
        return (block_start, key_piece[:, :, :HEAD], key_piece[:, :, HEAD:])

    def max_step(block_index, loop_carry):
        block_start, keys_block, values_block = take_block(block_index)

        def max_update(run_state):
            prior_max, prior_sum = run_state
            scores, allowed = block_scores(
                queries, keys_block, block_start, first_position, score_scale
            )
            masked = jnp.where(allowed, scores, -jnp.inf)
            new_max = jnp.maximum(prior_max, jnp.max(masked, axis=3))
            new_sum = prior_sum * jnp.exp(prior_max - new_max) + jnp.sum(
                jnp.exp(masked - new_max[..., None]), axis=3
            )
            return (new_max, new_sum)

        return lax.cond(block_start <= last_position, max_update, keep_state, loop_carry)

    stat_shape = (seq_count, HEADS, shard_len)
    run_max, run_sum = lax.fori_loop(
        0,
        block_count,
        max_step,
        (jnp.full(stat_shape, -jnp.inf, jnp.float32), jnp.zeros(stat_shape, jnp.float32)),
    )
    log_total = run_max + jnp.log(run_sum)

    def context_step(block_index, loop_carry):
        block_start, keys_block, values_block = take_block(block_index)

        def context_update(running_total):
            scores, allowed = block_scores(
                queries, keys_block, block_start, first_position, score_scale
            )
            exact_probs = jnp.where(allowed, jnp.exp(scores - log_total[..., None]), 0.0)
            return running_total + jnp.einsum(
                "shpr,srd->sphd",
                exact_probs.astype(jnp.bfloat16),
                values_block,
                preferred_element_type=jnp.float32,
            )

        return lax.cond(block_start <= last_position, context_update, keep_state, loop_carry)

    context = lax.fori_loop(
        0, block_count, context_step, jnp.zeros((seq_count, shard_len, HEADS, HEAD), jnp.float32)
    )
    sigmoid_gate = jax.nn.sigmoid(gate_logits.astype(jnp.float32)).reshape(
        seq_count, shard_len, HEADS, HEAD
    )
    upstream = gated_grad.astype(jnp.float32).reshape(seq_count, shard_len, HEADS, HEAD)
    context_grad = (upstream * sigmoid_gate).astype(jnp.bfloat16)
    gate_grad = (
        (upstream * context * sigmoid_gate * (1.0 - sigmoid_gate))
        .astype(jnp.bfloat16)
        .reshape(seq_count, shard_len, row_width)
    )
    grad_dot = jnp.transpose(jnp.sum(context_grad.astype(jnp.float32) * context, axis=3), (0, 2, 1))

    def grad_step(block_index, loop_carry):
        block_start, keys_block, values_block = take_block(block_index)

        def grad_update(run_state):
            query_total, pair_buffer = run_state
            scores, allowed = block_scores(
                queries, keys_block, block_start, first_position, score_scale
            )
            exact_probs = jnp.where(allowed, jnp.exp(scores - log_total[..., None]), 0.0)
            probs_low = exact_probs.astype(jnp.bfloat16)
            prob_grad = jnp.einsum(
                "sphd,srd->shpr", context_grad, values_block, preferred_element_type=jnp.float32
            )
            score_grad = (exact_probs * (prob_grad - grad_dot[..., None]) * score_scale).astype(
                jnp.bfloat16
            )
            query_total = query_total + jnp.einsum(
                "shpr,srd->sphd", score_grad, keys_block, preferred_element_type=jnp.float32
            )
            key_part = jnp.einsum(
                "shpr,sphd->srd", score_grad, queries, preferred_element_type=jnp.float32
            ).astype(jnp.bfloat16)
            value_part = jnp.einsum(
                "shpr,sphd->srd", probs_low, context_grad, preferred_element_type=jnp.float32
            ).astype(jnp.bfloat16)
            pair_block = jnp.concatenate([key_part, value_part], axis=2)
            pair_block = jnp.moveaxis(
                pair_block.reshape(seq_count, shards_per_block, shard_len, 2 * HEAD), 1, 0
            )
            pair_buffer = lax.dynamic_update_slice_in_dim(
                pair_buffer, pair_block, block_start // shard_len, 0
            )
            return (query_total, pair_buffer)

        return lax.cond(block_start <= last_position, grad_update, keep_state, loop_carry)

    query_total, pair_buffer = lax.fori_loop(
        0,
        block_count,
        grad_step,
        (
            jnp.zeros((seq_count, shard_len, HEADS, HEAD), jnp.float32),
            jnp.zeros((devices, seq_count, shard_len, 2 * HEAD), jnp.bfloat16),
        ),
    )
    query_grad = query_total.astype(jnp.bfloat16).reshape(seq_count, shard_len, row_width)
    token_count, model_width = moe_input.shape
    live_slot = routes < devices
    has_live = jnp.any(live_slot, axis=1)
    live_expert = jnp.sum(jnp.where(live_slot, routes, 0), axis=1)
    token_weight = jnp.sum(jnp.where(live_slot, route_weights.astype(jnp.float32), 0.0), axis=1)
    member = (live_expert[:, None] == jnp.arange(devices)[None, :]) & has_live[:, None]
    earlier = (jnp.arange(token_count)[None, :] < jnp.arange(token_count)[:, None]).astype(
        jnp.bfloat16
    )
    before = jnp.dot(earlier, member.astype(jnp.bfloat16), preferred_element_type=jnp.float32)
    slot_rank = jnp.sum(jnp.where(member, before, 0.0), axis=1)
    placed = member.T[:, None, :] & (
        slot_rank[None, None, :] == jnp.arange(CAP)[None, :, None].astype(jnp.float32)
    )
    dispatch_mat = placed.reshape(devices * CAP, token_count).astype(jnp.bfloat16)
    model_cols = model_width
    pad_cols = 128
    rows_send = (
        jnp.dot(dispatch_mat, moe_input, preferred_element_type=jnp.float32)
        .astype(jnp.bfloat16)
        .reshape(devices, CAP, model_width)
    )
    grads_send = (
        jnp.dot(dispatch_mat, out_grad, preferred_element_type=jnp.float32)
        .astype(jnp.bfloat16)
        .reshape(devices, CAP, model_width)
    )
    weights_send = jnp.sum(jnp.where(placed, token_weight[None, None, :], 0.0), axis=2).astype(
        jnp.bfloat16
    )
    send_all = jnp.concatenate(
        [
            rows_send,
            grads_send,
            jnp.broadcast_to(weights_send[:, :, None], (devices, CAP, pad_cols)),
        ],
        axis=2,
    )
    hidden_cols = gate_proj.shape[2]
    weight_cat = jnp.concatenate(
        [gate_proj, up_proj, jnp.transpose(down_proj, (0, 2, 1))], axis=2
    )
    weight_full = lax.all_gather(weight_cat, "dp", axis=1, tiled=True)[0]
    gate_mat = weight_full[:, :hidden_cols]
    up_mat = weight_full[:, hidden_cols : 2 * hidden_cols]
    down_mat = jnp.transpose(weight_full[:, 2 * hidden_cols :])
    recv_all = lax.all_to_all(send_all, "expert", split_axis=0, concat_axis=0, tiled=True)
    rows_in = recv_all[:, :, :model_cols]
    grads_in = recv_all[:, :, model_cols : 2 * model_cols]
    weights_in = recv_all[:, :, 2 * model_cols]
    flat_rows = rows_in.reshape(devices * CAP, model_width)
    flat_grads = grads_in.reshape(devices * CAP, model_width)
    gate_pre = jnp.dot(flat_rows, gate_mat, preferred_element_type=jnp.float32)
    up_pre = jnp.dot(flat_rows, up_mat, preferred_element_type=jnp.float32)
    sigmoid_pre = jax.nn.sigmoid(gate_pre)
    silu_value = gate_pre * sigmoid_pre
    hidden = (silu_value * up_pre).astype(jnp.bfloat16)
    expert_out = jnp.dot(hidden, down_mat, preferred_element_type=jnp.float32)
    weight_back = jnp.sum(expert_out * flat_grads.astype(jnp.float32), axis=1).astype(jnp.bfloat16)
    scaled_grad = (
        weights_in.reshape(-1)[:, None].astype(jnp.float32) * flat_grads.astype(jnp.float32)
    ).astype(jnp.bfloat16)
    contract_last = (((1,), (1,)), ((), ()))
    hidden_grad = lax.dot_general(
        scaled_grad, down_mat, contract_last, preferred_element_type=jnp.float32
    )
    slope = sigmoid_pre * (1.0 + gate_pre * (1.0 - sigmoid_pre))
    gate_rows = (hidden_grad * up_pre * slope).astype(jnp.bfloat16)
    up_rows = (hidden_grad * silu_value).astype(jnp.bfloat16)
    input_rows = (
        lax.dot_general(gate_rows, gate_mat, contract_last, preferred_element_type=jnp.float32)
        + lax.dot_general(up_rows, up_mat, contract_last, preferred_element_type=jnp.float32)
    ).astype(jnp.bfloat16)
    hidden_width = hidden.shape[1]
    contract_first = (((0,), (0,)), ((), ()))
    summed = lax.psum_scatter(
        jnp.concatenate(
            [
                lax.dot_general(
                    flat_rows, gate_rows, contract_first, preferred_element_type=jnp.float32
                ),
                lax.dot_general(
                    flat_rows, up_rows, contract_first, preferred_element_type=jnp.float32
                ),
                lax.dot_general(
                    scaled_grad, hidden, contract_first, preferred_element_type=jnp.float32
                ),
            ],
            axis=1,
        ).astype(jnp.bfloat16),
        "dp",
        scatter_dimension=0,
        tiled=True,
    ).astype(jnp.float32)
    gate_proj_grad = summed[:, :hidden_width][None]
    up_proj_grad = summed[:, hidden_width : 2 * hidden_width][None]
    down_proj_grad = jnp.transpose(summed[:, 2 * hidden_width :])[None]
    pair_total = lax.psum_scatter(pair_buffer, "expert", scatter_dimension=0, tiled=True)[0]
    key_grad = pair_total[:, :, :HEAD]
    value_grad = pair_total[:, :, HEAD:]
    back_all = lax.all_to_all(
        jnp.concatenate(
            [
                input_rows.reshape(devices, CAP, model_width),
                jnp.broadcast_to(weight_back.reshape(devices, CAP, 1), (devices, CAP, pad_cols)),
            ],
            axis=2,
        ),
        "expert",
        split_axis=0,
        concat_axis=0,
        tiled=True,
    )
    input_back = back_all[:, :, :model_width]
    weights_back = back_all[:, :, model_width]
    input_grad = lax.dot_general(
        dispatch_mat,
        input_back.reshape(devices * CAP, model_width),
        contract_first,
        preferred_element_type=jnp.float32,
    ).astype(jnp.bfloat16)
    token_back = jnp.sum(
        dispatch_mat.astype(jnp.float32) * weights_back.reshape(-1).astype(jnp.float32)[:, None],
        axis=0,
    )
    route_grad = jnp.where(live_slot, token_back[:, None], 0.0).astype(jnp.bfloat16)
    return (
        query_grad,
        key_grad,
        value_grad,
        gate_grad,
        input_grad,
        route_grad,
        gate_proj_grad,
        up_proj_grad,
        down_proj_grad,
    )


def solution(mesh):
    return jax.shard_map(
        shards,
        mesh=mesh,
        in_specs=(
            P("dp", "expert", None),
            P("dp", "expert", None),
            P("dp", "expert", None),
            P("dp", "expert", None),
            P("dp", "expert", None),
            P(("dp", "expert"), None),
            P(("dp", "expert"), None),
            P(("dp", "expert"), None),
            P(("dp", "expert"), None),
            P("expert", "dp", None),
            P("expert", "dp", None),
            P("expert", None, "dp"),
        ),
        out_specs=(
            P("dp", "expert", None),
            P("dp", "expert", None),
            P("dp", "expert", None),
            P("dp", "expert", None),
            P(("dp", "expert"), None),
            P(("dp", "expert"), None),
            P("expert", "dp", None),
            P("expert", "dp", None),
            P("expert", None, "dp"),
        ),
        check_vma=False,
    )
```

```python
import jax
import jax.numpy as jnp
from jax import lax
from jax.sharding import PartitionSpec as P

HEADS = 8
HEAD = 256
CAP = 2


def shards(
    query_rows,
    key_rows,
    value_rows,
    gate_logits,
    gated_grad,
    moe_input,
    out_grad,
    routes,
    route_weights,
    gate_proj,
    up_proj,
    down_proj,
):
    seq_count, shard_len, row_width = query_rows.shape
    devices = lax.axis_size("expert")
    position = lax.axis_index("expert")
    first_position = position * shard_len
    last_position = first_position + shard_len - 1
    total_len = shard_len * devices
    score_scale = HEAD ** (-0.5)
    queries = query_rows.reshape(seq_count, shard_len, HEADS, HEAD)
    packed = jnp.concatenate([key_rows, value_rows], axis=2)
    gathered = lax.all_gather(packed, "expert", axis=1, tiled=True)

    keys_all = gathered[:, :, :HEAD]
    values_all = gathered[:, :, HEAD:]
    scores = (
        jnp.einsum("sphd,srd->shpr", queries, keys_all, preferred_element_type=jnp.float32)
        * score_scale
    )
    query_pos = first_position + jnp.arange(shard_len)
    key_pos = jnp.arange(total_len)
    allowed = (key_pos[None, :] <= query_pos[:, None])[None, None]
    masked = jnp.where(allowed, scores, -jnp.inf)
    row_max = jnp.max(masked, axis=3, keepdims=True)
    log_total = row_max + jnp.log(jnp.sum(jnp.exp(masked - row_max), axis=3, keepdims=True))
    exact_probs = jnp.where(allowed, jnp.exp(scores - log_total), 0.0)
    probs_low = exact_probs.astype(jnp.bfloat16)
    context = jnp.einsum(
        "shpr,srd->sphd", probs_low, values_all, preferred_element_type=jnp.float32
    )
    sigmoid_gate = jax.nn.sigmoid(gate_logits.astype(jnp.float32)).reshape(
        seq_count, shard_len, HEADS, HEAD
    )
    upstream = gated_grad.astype(jnp.float32).reshape(seq_count, shard_len, HEADS, HEAD)
    context_grad = (upstream * sigmoid_gate).astype(jnp.bfloat16)
    gate_grad = (
        (upstream * context * sigmoid_gate * (1.0 - sigmoid_gate))
        .astype(jnp.bfloat16)
        .reshape(seq_count, shard_len, row_width)
    )
    grad_dot = jnp.transpose(jnp.sum(context_grad.astype(jnp.float32) * context, axis=3), (0, 2, 1))
    prob_grad = jnp.einsum(
        "sphd,srd->shpr", context_grad, values_all, preferred_element_type=jnp.float32
    )
    score_grad = (exact_probs * (prob_grad - grad_dot[..., None]) * score_scale).astype(
        jnp.bfloat16
    )
    query_total = jnp.einsum(
        "shpr,srd->sphd", score_grad, keys_all, preferred_element_type=jnp.float32
    )
    key_part = jnp.einsum(
        "shpr,sphd->srd", score_grad, queries, preferred_element_type=jnp.float32
    ).astype(jnp.bfloat16)
    value_part = jnp.einsum(
        "shpr,sphd->srd", probs_low, context_grad, preferred_element_type=jnp.float32
    ).astype(jnp.bfloat16)
    pair_buffer = lax.optimization_barrier(
        jnp.moveaxis(
            jnp.concatenate([key_part, value_part], axis=2).reshape(
                seq_count, devices, shard_len, 2 * HEAD
            ),
            1,
            0,
        )
    )
    query_grad = query_total.astype(jnp.bfloat16).reshape(seq_count, shard_len, row_width)
    token_count, model_width = moe_input.shape
    live_slot = routes < devices
    has_live = jnp.any(live_slot, axis=1)
    live_expert = jnp.sum(jnp.where(live_slot, routes, 0), axis=1)
    token_weight = jnp.sum(jnp.where(live_slot, route_weights.astype(jnp.float32), 0.0), axis=1)
    member = (live_expert[:, None] == jnp.arange(devices)[None, :]) & has_live[:, None]
    earlier = (jnp.arange(token_count)[None, :] < jnp.arange(token_count)[:, None]).astype(
        jnp.bfloat16
    )
    before = jnp.dot(earlier, member.astype(jnp.bfloat16), preferred_element_type=jnp.float32)
    slot_rank = jnp.sum(jnp.where(member, before, 0.0), axis=1)
    placed = member.T[:, None, :] & (
        slot_rank[None, None, :] == jnp.arange(CAP)[None, :, None].astype(jnp.float32)
    )
    dispatch_mat = placed.reshape(devices * CAP, token_count).astype(jnp.bfloat16)
    model_cols = model_width
    pad_cols = 128
    rows_send = (
        jnp.dot(dispatch_mat, moe_input, preferred_element_type=jnp.float32)
        .astype(jnp.bfloat16)
        .reshape(devices, CAP, model_width)
    )
    grads_send = (
        jnp.dot(dispatch_mat, out_grad, preferred_element_type=jnp.float32)
        .astype(jnp.bfloat16)
        .reshape(devices, CAP, model_width)
    )
    weights_send = jnp.sum(jnp.where(placed, token_weight[None, None, :], 0.0), axis=2).astype(
        jnp.bfloat16
    )
    send_all = jnp.concatenate(
        [
            rows_send,
            grads_send,
            jnp.broadcast_to(weights_send[:, :, None], (devices, CAP, pad_cols)),
        ],
        axis=2,
    )
    hidden_cols = gate_proj.shape[2]
    weight_cat = jnp.concatenate(
        [gate_proj, up_proj, jnp.transpose(down_proj, (0, 2, 1))], axis=2
    )
    weight_full = lax.all_gather(weight_cat, "dp", axis=1, tiled=True)[0]
    gate_mat = weight_full[:, :hidden_cols]
    up_mat = weight_full[:, hidden_cols : 2 * hidden_cols]
    down_mat = jnp.transpose(weight_full[:, 2 * hidden_cols :])
    recv_all = lax.all_to_all(send_all, "expert", split_axis=0, concat_axis=0, tiled=True)
    rows_in = recv_all[:, :, :model_cols]
    grads_in = recv_all[:, :, model_cols : 2 * model_cols]
    weights_in = recv_all[:, :, 2 * model_cols]
    flat_rows = rows_in.reshape(devices * CAP, model_width)
    flat_grads = grads_in.reshape(devices * CAP, model_width)
    gate_pre = jnp.dot(flat_rows, gate_mat, preferred_element_type=jnp.float32)
    up_pre = jnp.dot(flat_rows, up_mat, preferred_element_type=jnp.float32)
    sigmoid_pre = jax.nn.sigmoid(gate_pre)
    silu_value = gate_pre * sigmoid_pre
    hidden = (silu_value * up_pre).astype(jnp.bfloat16)
    expert_out = jnp.dot(hidden, down_mat, preferred_element_type=jnp.float32)
    weight_back = jnp.sum(expert_out * flat_grads.astype(jnp.float32), axis=1).astype(jnp.bfloat16)
    scaled_grad = (
        weights_in.reshape(-1)[:, None].astype(jnp.float32) * flat_grads.astype(jnp.float32)
    ).astype(jnp.bfloat16)
    contract_last = (((1,), (1,)), ((), ()))
    hidden_grad = lax.dot_general(
        scaled_grad, down_mat, contract_last, preferred_element_type=jnp.float32
    )
    slope = sigmoid_pre * (1.0 + gate_pre * (1.0 - sigmoid_pre))
    gate_rows = (hidden_grad * up_pre * slope).astype(jnp.bfloat16)
    up_rows = (hidden_grad * silu_value).astype(jnp.bfloat16)
    input_rows = (
        lax.dot_general(gate_rows, gate_mat, contract_last, preferred_element_type=jnp.float32)
        + lax.dot_general(up_rows, up_mat, contract_last, preferred_element_type=jnp.float32)
    ).astype(jnp.bfloat16)
    hidden_width = hidden.shape[1]
    contract_first = (((0,), (0,)), ((), ()))
    summed = lax.psum_scatter(
        jnp.concatenate(
            [
                lax.dot_general(
                    flat_rows, gate_rows, contract_first, preferred_element_type=jnp.float32
                ),
                lax.dot_general(
                    flat_rows, up_rows, contract_first, preferred_element_type=jnp.float32
                ),
                lax.dot_general(
                    scaled_grad, hidden, contract_first, preferred_element_type=jnp.float32
                ),
            ],
            axis=1,
        ).astype(jnp.bfloat16),
        "dp",
        scatter_dimension=0,
        tiled=True,
    ).astype(jnp.float32)
    gate_proj_grad = summed[:, :hidden_width][None]
    up_proj_grad = summed[:, hidden_width : 2 * hidden_width][None]
    down_proj_grad = jnp.transpose(summed[:, 2 * hidden_width :])[None]
    pair_total = lax.psum_scatter(pair_buffer, "expert", scatter_dimension=0, tiled=True)[0]
    key_grad = pair_total[:, :, :HEAD]
    value_grad = pair_total[:, :, HEAD:]
    back_all = lax.all_to_all(
        jnp.concatenate(
            [
                input_rows.reshape(devices, CAP, model_width),
                jnp.broadcast_to(weight_back.reshape(devices, CAP, 1), (devices, CAP, pad_cols)),
            ],
            axis=2,
        ),
        "expert",
        split_axis=0,
        concat_axis=0,
        tiled=True,
    )
    input_back = back_all[:, :, :model_width]
    weights_back = back_all[:, :, model_width]
    input_grad = lax.dot_general(
        dispatch_mat,
        input_back.reshape(devices * CAP, model_width),
        contract_first,
        preferred_element_type=jnp.float32,
    ).astype(jnp.bfloat16)
    token_back = jnp.sum(
        dispatch_mat.astype(jnp.float32) * weights_back.reshape(-1).astype(jnp.float32)[:, None],
        axis=0,
    )
    route_grad = jnp.where(live_slot, token_back[:, None], 0.0).astype(jnp.bfloat16)
    return (
        query_grad,
        key_grad,
        value_grad,
        gate_grad,
        input_grad,
        route_grad,
        gate_proj_grad,
        up_proj_grad,
        down_proj_grad,
    )


def solution(mesh):
    return jax.shard_map(
        shards,
        mesh=mesh,
        in_specs=(
            P("dp", "expert", None),
            P("dp", "expert", None),
            P("dp", "expert", None),
            P("dp", "expert", None),
            P("dp", "expert", None),
            P(("dp", "expert"), None),
            P(("dp", "expert"), None),
            P(("dp", "expert"), None),
            P(("dp", "expert"), None),
            P("expert", "dp", None),
            P("expert", "dp", None),
            P("expert", None, "dp"),
        ),
        out_specs=(
            P("dp", "expert", None),
            P("dp", "expert", None),
            P("dp", "expert", None),
            P("dp", "expert", None),
            P(("dp", "expert"), None),
            P(("dp", "expert"), None),
            P("expert", "dp", None),
            P("expert", "dp", None),
            P("expert", None, "dp"),
        ),
        check_vma=False,
    )
```

```python
import jax
import jax.numpy as jnp
from jax import lax
from jax.experimental import pallas as pl
from jax.experimental.pallas import tpu as pltpu
from jax.sharding import PartitionSpec as P

HEADS = 8
HEAD = 256
CAP = 2


def pair_return_kernel(parts_ref, out_ref, landing, send_sems, recv_sems):
    devices = parts_ref.shape[0]
    me = lax.axis_index("expert")
    row = lax.axis_index("dp")
    mesh_ids = pl.DeviceIdType.MESH

    def peer_copy(block, slot, peer):
        return pltpu.make_async_remote_copy(
            src_ref=parts_ref.at[block],
            dst_ref=landing.at[slot],
            send_sem=send_sems.at[block],
            recv_sem=recv_sems.at[slot],
            device_id=(row, peer),
            device_id_type=mesh_ids,
        )

    barrier = pltpu.get_barrier_semaphore()

    def greet(step, carry):
        peer = lax.rem(me + 1 + step, devices)
        pl.semaphore_signal(barrier, inc=1, device_id=(row, peer), device_id_type=mesh_ids)
        return carry

    lax.fori_loop(0, devices - 1, greet, 0)
    pl.semaphore_wait(barrier, devices - 1)

    def send(block, carry):
        peer_copy(block, me, block).start()
        return carry

    lax.fori_loop(0, me, send, 0)

    def receive(source, total):
        peer_copy(source, source, source).wait_recv()
        return total + landing[source].astype(jnp.float32)

    total = lax.fori_loop(me + 1, devices, receive, parts_ref[me].astype(jnp.float32))
    out_ref[...] = total.astype(out_ref.dtype)

    def finish(block, carry):
        peer_copy(block, me, block).wait_send()
        return carry

    lax.fori_loop(0, me, finish, 0)


def pair_return(pair_buffer):
    devices = pair_buffer.shape[0]
    return pl.pallas_call(
        pair_return_kernel,
        out_shape=jax.ShapeDtypeStruct(pair_buffer.shape[1:], pair_buffer.dtype),
        in_specs=[pl.BlockSpec(memory_space=pltpu.VMEM)],
        out_specs=pl.BlockSpec(memory_space=pltpu.VMEM),
        scratch_shapes=[
            pltpu.VMEM(pair_buffer.shape, pair_buffer.dtype),
            pltpu.SemaphoreType.DMA((devices,)),
            pltpu.SemaphoreType.DMA((devices,)),
        ],
        compiler_params=pltpu.CompilerParams(collective_id=0, has_side_effects=True),
    )(pair_buffer)


def shards(
    query_rows,
    key_rows,
    value_rows,
    gate_logits,
    gated_grad,
    moe_input,
    out_grad,
    routes,
    route_weights,
    gate_proj,
    up_proj,
    down_proj,
):
    seq_count, shard_len, row_width = query_rows.shape
    devices = lax.axis_size("expert")
    position = lax.axis_index("expert")
    first_position = position * shard_len
    last_position = first_position + shard_len - 1
    total_len = shard_len * devices
    score_scale = HEAD ** (-0.5)
    queries = query_rows.reshape(seq_count, shard_len, HEADS, HEAD)
    packed = jnp.concatenate([key_rows, value_rows], axis=2)
    gathered = lax.all_gather(packed, "expert", axis=1, tiled=True)

    keys_all = gathered[:, :, :HEAD]
    values_all = gathered[:, :, HEAD:]
    scores = (
        jnp.einsum("sphd,srd->shpr", queries, keys_all, preferred_element_type=jnp.float32)
        * score_scale
    )
    query_pos = first_position + jnp.arange(shard_len)
    key_pos = jnp.arange(total_len)
    allowed = (key_pos[None, :] <= query_pos[:, None])[None, None]
    masked = jnp.where(allowed, scores, -jnp.inf)
    row_max = jnp.max(masked, axis=3, keepdims=True)
    log_total = row_max + jnp.log(jnp.sum(jnp.exp(masked - row_max), axis=3, keepdims=True))
    exact_probs = jnp.where(allowed, jnp.exp(scores - log_total), 0.0)
    probs_low = exact_probs.astype(jnp.bfloat16)
    context = jnp.einsum(
        "shpr,srd->sphd", probs_low, values_all, preferred_element_type=jnp.float32
    )
    sigmoid_gate = jax.nn.sigmoid(gate_logits.astype(jnp.float32)).reshape(
        seq_count, shard_len, HEADS, HEAD
    )
    upstream = gated_grad.astype(jnp.float32).reshape(seq_count, shard_len, HEADS, HEAD)
    context_grad = (upstream * sigmoid_gate).astype(jnp.bfloat16)
    gate_grad = (
        (upstream * context * sigmoid_gate * (1.0 - sigmoid_gate))
        .astype(jnp.bfloat16)
        .reshape(seq_count, shard_len, row_width)
    )
    grad_dot = jnp.transpose(jnp.sum(context_grad.astype(jnp.float32) * context, axis=3), (0, 2, 1))
    prob_grad = jnp.einsum(
        "sphd,srd->shpr", context_grad, values_all, preferred_element_type=jnp.float32
    )
    score_grad = (exact_probs * (prob_grad - grad_dot[..., None]) * score_scale).astype(
        jnp.bfloat16
    )
    query_total = jnp.einsum(
        "shpr,srd->sphd", score_grad, keys_all, preferred_element_type=jnp.float32
    )
    key_part = jnp.einsum(
        "shpr,sphd->srd", score_grad, queries, preferred_element_type=jnp.float32
    ).astype(jnp.bfloat16)
    value_part = jnp.einsum(
        "shpr,sphd->srd", probs_low, context_grad, preferred_element_type=jnp.float32
    ).astype(jnp.bfloat16)
    pair_buffer = (
        jnp.moveaxis(
            jnp.concatenate([key_part, value_part], axis=2).reshape(
                seq_count, devices, shard_len, 2 * HEAD
            ),
            1,
            0,
        )
    )
    query_grad = query_total.astype(jnp.bfloat16).reshape(seq_count, shard_len, row_width)
    token_count, model_width = moe_input.shape
    live_slot = routes < devices
    has_live = jnp.any(live_slot, axis=1)
    live_expert = jnp.sum(jnp.where(live_slot, routes, 0), axis=1)
    token_weight = jnp.sum(jnp.where(live_slot, route_weights.astype(jnp.float32), 0.0), axis=1)
    member = (live_expert[:, None] == jnp.arange(devices)[None, :]) & has_live[:, None]
    earlier = (jnp.arange(token_count)[None, :] < jnp.arange(token_count)[:, None]).astype(
        jnp.bfloat16
    )
    before = jnp.dot(earlier, member.astype(jnp.bfloat16), preferred_element_type=jnp.float32)
    slot_rank = jnp.sum(jnp.where(member, before, 0.0), axis=1)
    placed = member.T[:, None, :] & (
        slot_rank[None, None, :] == jnp.arange(CAP)[None, :, None].astype(jnp.float32)
    )
    dispatch_mat = placed.reshape(devices * CAP, token_count).astype(jnp.bfloat16)
    model_cols = model_width
    pad_cols = 128
    rows_send = (
        jnp.dot(dispatch_mat, moe_input, preferred_element_type=jnp.float32)
        .astype(jnp.bfloat16)
        .reshape(devices, CAP, model_width)
    )
    grads_send = (
        jnp.dot(dispatch_mat, out_grad, preferred_element_type=jnp.float32)
        .astype(jnp.bfloat16)
        .reshape(devices, CAP, model_width)
    )
    weights_send = jnp.sum(jnp.where(placed, token_weight[None, None, :], 0.0), axis=2).astype(
        jnp.bfloat16
    )
    send_all = jnp.concatenate(
        [
            rows_send,
            grads_send,
            jnp.broadcast_to(weights_send[:, :, None], (devices, CAP, pad_cols)),
        ],
        axis=2,
    )
    hidden_cols = gate_proj.shape[2]
    weight_cat = jnp.concatenate(
        [gate_proj, up_proj, jnp.transpose(down_proj, (0, 2, 1))], axis=2
    )
    weight_full = lax.all_gather(weight_cat, "dp", axis=1, tiled=True)[0]
    gate_mat = weight_full[:, :hidden_cols]
    up_mat = weight_full[:, hidden_cols : 2 * hidden_cols]
    down_mat = jnp.transpose(weight_full[:, 2 * hidden_cols :])
    recv_all = lax.all_to_all(send_all, "expert", split_axis=0, concat_axis=0, tiled=True)
    rows_in = recv_all[:, :, :model_cols]
    grads_in = recv_all[:, :, model_cols : 2 * model_cols]
    weights_in = recv_all[:, :, 2 * model_cols]
    flat_rows = rows_in.reshape(devices * CAP, model_width)
    flat_grads = grads_in.reshape(devices * CAP, model_width)
    gate_pre = jnp.dot(flat_rows, gate_mat, preferred_element_type=jnp.float32)
    up_pre = jnp.dot(flat_rows, up_mat, preferred_element_type=jnp.float32)
    sigmoid_pre = jax.nn.sigmoid(gate_pre)
    silu_value = gate_pre * sigmoid_pre
    hidden = (silu_value * up_pre).astype(jnp.bfloat16)
    expert_out = jnp.dot(hidden, down_mat, preferred_element_type=jnp.float32)
    weight_back = jnp.sum(expert_out * flat_grads.astype(jnp.float32), axis=1).astype(jnp.bfloat16)
    scaled_grad = (
        weights_in.reshape(-1)[:, None].astype(jnp.float32) * flat_grads.astype(jnp.float32)
    ).astype(jnp.bfloat16)
    contract_last = (((1,), (1,)), ((), ()))
    hidden_grad = lax.dot_general(
        scaled_grad, down_mat, contract_last, preferred_element_type=jnp.float32
    )
    slope = sigmoid_pre * (1.0 + gate_pre * (1.0 - sigmoid_pre))
    gate_rows = (hidden_grad * up_pre * slope).astype(jnp.bfloat16)
    up_rows = (hidden_grad * silu_value).astype(jnp.bfloat16)
    input_rows = (
        lax.dot_general(gate_rows, gate_mat, contract_last, preferred_element_type=jnp.float32)
        + lax.dot_general(up_rows, up_mat, contract_last, preferred_element_type=jnp.float32)
    ).astype(jnp.bfloat16)
    hidden_width = hidden.shape[1]
    contract_first = (((0,), (0,)), ((), ()))
    summed = lax.psum_scatter(
        jnp.concatenate(
            [
                lax.dot_general(
                    flat_rows, gate_rows, contract_first, preferred_element_type=jnp.float32
                ),
                lax.dot_general(
                    flat_rows, up_rows, contract_first, preferred_element_type=jnp.float32
                ),
                lax.dot_general(
                    scaled_grad, hidden, contract_first, preferred_element_type=jnp.float32
                ),
            ],
            axis=1,
        ).astype(jnp.bfloat16),
        "dp",
        scatter_dimension=0,
        tiled=True,
    ).astype(jnp.float32)
    gate_proj_grad = summed[:, :hidden_width][None]
    up_proj_grad = summed[:, hidden_width : 2 * hidden_width][None]
    down_proj_grad = jnp.transpose(summed[:, 2 * hidden_width :])[None]
    pair_total = pair_return(pair_buffer)
    key_grad = pair_total[:, :, :HEAD]
    value_grad = pair_total[:, :, HEAD:]
    back_all = lax.all_to_all(
        jnp.concatenate(
            [
                input_rows.reshape(devices, CAP, model_width),
                jnp.broadcast_to(weight_back.reshape(devices, CAP, 1), (devices, CAP, pad_cols)),
            ],
            axis=2,
        ),
        "expert",
        split_axis=0,
        concat_axis=0,
        tiled=True,
    )
    input_back = back_all[:, :, :model_width]
    weights_back = back_all[:, :, model_width]
    input_grad = lax.dot_general(
        dispatch_mat,
        input_back.reshape(devices * CAP, model_width),
        contract_first,
        preferred_element_type=jnp.float32,
    ).astype(jnp.bfloat16)
    token_back = jnp.sum(
        dispatch_mat.astype(jnp.float32) * weights_back.reshape(-1).astype(jnp.float32)[:, None],
        axis=0,
    )
    route_grad = jnp.where(live_slot, token_back[:, None], 0.0).astype(jnp.bfloat16)
    return (
        query_grad,
        key_grad,
        value_grad,
        gate_grad,
        input_grad,
        route_grad,
        gate_proj_grad,
        up_proj_grad,
        down_proj_grad,
    )


def solution(mesh):
    return jax.shard_map(
        shards,
        mesh=mesh,
        in_specs=(
            P("dp", "expert", None),
            P("dp", "expert", None),
            P("dp", "expert", None),
            P("dp", "expert", None),
            P("dp", "expert", None),
            P(("dp", "expert"), None),
            P(("dp", "expert"), None),
            P(("dp", "expert"), None),
            P(("dp", "expert"), None),
            P("expert", "dp", None),
            P("expert", "dp", None),
            P("expert", None, "dp"),
        ),
        out_specs=(
            P("dp", "expert", None),
            P("dp", "expert", None),
            P("dp", "expert", None),
            P("dp", "expert", None),
            P(("dp", "expert"), None),
            P(("dp", "expert"), None),
            P("expert", "dp", None),
            P("expert", "dp", None),
            P("expert", None, "dp"),
        ),
        check_vma=False,
    )
```

```python
import jax
import jax.numpy as jnp
from jax import lax
from jax.experimental import pallas as pl
from jax.experimental.pallas import tpu as pltpu
from jax.sharding import PartitionSpec as P

HEADS = 8
HEAD = 256
CAP = 2
CHAIN_DTYPE = jnp.float32


def pair_chain_kernel(parts_ref, out_ref, sendbuf, recvbuf, send_sems, recv_sems):
    devices, seqs = parts_ref.shape[0], parts_ref.shape[1]
    me = lax.axis_index("expert")
    row = lax.axis_index("dp")
    mesh_ids = pl.DeviceIdType.MESH
    has_upper = me < devices - 1
    is_top = me == devices - 1
    upper = lax.rem(me + 1, devices)
    lower = lax.rem(me + devices - 1, devices)

    def link(block, seq, peer):
        return pltpu.make_async_remote_copy(
            src_ref=sendbuf.at[block, seq],
            dst_ref=recvbuf.at[block, seq],
            send_sem=send_sems.at[block, seq],
            recv_sem=recv_sems.at[block, seq],
            device_id=(row, peer),
            device_id_type=mesh_ids,
        )

    barrier = pltpu.get_barrier_semaphore()
    for peer in (upper, lower):
        pl.semaphore_signal(barrier, inc=1, device_id=(row, peer), device_id_type=mesh_ids)
    pl.semaphore_wait(barrier, 2)

    for seq in range(seqs):

        @pl.when(has_upper)
        def _():
            link(me, seq, upper).wait_recv()
            out_ref[seq] = (
                parts_ref[me, seq].astype(jnp.float32) + recvbuf[me, seq].astype(jnp.float32)
            ).astype(out_ref.dtype)

        @pl.when(is_top)
        def _():
            out_ref[seq] = parts_ref[me, seq]

    def forward(step, carry):
        block = me - 1 - step
        for seq in range(seqs):

            @pl.when(has_upper)
            def _():
                link(block, seq, upper).wait_recv()
                sendbuf[block, seq] = (
                    parts_ref[block, seq].astype(jnp.float32)
                    + recvbuf[block, seq].astype(jnp.float32)
                ).astype(sendbuf.dtype)

            @pl.when(is_top)
            def _():
                sendbuf[block, seq] = parts_ref[block, seq].astype(sendbuf.dtype)

            link(block, seq, lower).start()
        return carry

    lax.fori_loop(0, me, forward, 0)

    def finish(step, carry):
        block = me - 1 - step
        for seq in range(seqs):
            link(block, seq, lower).wait_send()
        return carry

    lax.fori_loop(0, me, finish, 0)


def pair_return(pair_buffer):
    return pl.pallas_call(
        pair_chain_kernel,
        out_shape=jax.ShapeDtypeStruct(pair_buffer.shape[1:], pair_buffer.dtype),
        in_specs=[pl.BlockSpec(memory_space=pltpu.VMEM)],
        out_specs=pl.BlockSpec(memory_space=pltpu.VMEM),
        scratch_shapes=[
            pltpu.VMEM(pair_buffer.shape, CHAIN_DTYPE),
            pltpu.VMEM(pair_buffer.shape, CHAIN_DTYPE),
            pltpu.SemaphoreType.DMA(pair_buffer.shape[:2]),
            pltpu.SemaphoreType.DMA(pair_buffer.shape[:2]),
        ],
        compiler_params=pltpu.CompilerParams(collective_id=0, has_side_effects=True),
    )(pair_buffer)


def shards(
    query_rows,
    key_rows,
    value_rows,
    gate_logits,
    gated_grad,
    moe_input,
    out_grad,
    routes,
    route_weights,
    gate_proj,
    up_proj,
    down_proj,
):
    seq_count, shard_len, row_width = query_rows.shape
    devices = lax.axis_size("expert")
    position = lax.axis_index("expert")
    first_position = position * shard_len
    last_position = first_position + shard_len - 1
    total_len = shard_len * devices
    score_scale = HEAD ** (-0.5)
    queries = query_rows.reshape(seq_count, shard_len, HEADS, HEAD)
    packed = jnp.concatenate([key_rows, value_rows], axis=2)
    gathered = lax.all_gather(packed, "expert", axis=1, tiled=True)

    keys_all = gathered[:, :, :HEAD]
    values_all = gathered[:, :, HEAD:]
    scores = (
        jnp.einsum("sphd,srd->shpr", queries, keys_all, preferred_element_type=jnp.float32)
        * score_scale
    )
    query_pos = first_position + jnp.arange(shard_len)
    key_pos = jnp.arange(total_len)
    allowed = (key_pos[None, :] <= query_pos[:, None])[None, None]
    masked = jnp.where(allowed, scores, -jnp.inf)
    row_max = jnp.max(masked, axis=3, keepdims=True)
    log_total = row_max + jnp.log(jnp.sum(jnp.exp(masked - row_max), axis=3, keepdims=True))
    exact_probs = jnp.where(allowed, jnp.exp(scores - log_total), 0.0)
    probs_low = exact_probs.astype(jnp.bfloat16)
    context = jnp.einsum(
        "shpr,srd->sphd", probs_low, values_all, preferred_element_type=jnp.float32
    )
    sigmoid_gate = jax.nn.sigmoid(gate_logits.astype(jnp.float32)).reshape(
        seq_count, shard_len, HEADS, HEAD
    )
    upstream = gated_grad.astype(jnp.float32).reshape(seq_count, shard_len, HEADS, HEAD)
    context_grad = (upstream * sigmoid_gate).astype(jnp.bfloat16)
    gate_grad = (
        (upstream * context * sigmoid_gate * (1.0 - sigmoid_gate))
        .astype(jnp.bfloat16)
        .reshape(seq_count, shard_len, row_width)
    )
    grad_dot = jnp.transpose(jnp.sum(context_grad.astype(jnp.float32) * context, axis=3), (0, 2, 1))
    prob_grad = jnp.einsum(
        "sphd,srd->shpr", context_grad, values_all, preferred_element_type=jnp.float32
    )
    score_grad = (exact_probs * (prob_grad - grad_dot[..., None]) * score_scale).astype(
        jnp.bfloat16
    )
    query_total = jnp.einsum(
        "shpr,srd->sphd", score_grad, keys_all, preferred_element_type=jnp.float32
    )
    key_part = jnp.einsum(
        "shpr,sphd->srd", score_grad, queries, preferred_element_type=jnp.float32
    ).astype(jnp.bfloat16)
    value_part = jnp.einsum(
        "shpr,sphd->srd", probs_low, context_grad, preferred_element_type=jnp.float32
    ).astype(jnp.bfloat16)
    pair_buffer = (
        jnp.moveaxis(
            jnp.concatenate([key_part, value_part], axis=2).reshape(
                seq_count, devices, shard_len, 2 * HEAD
            ),
            1,
            0,
        )
    )
    query_grad = query_total.astype(jnp.bfloat16).reshape(seq_count, shard_len, row_width)
    token_count, model_width = moe_input.shape
    live_slot = routes < devices
    has_live = jnp.any(live_slot, axis=1)
    live_expert = jnp.sum(jnp.where(live_slot, routes, 0), axis=1)
    token_weight = jnp.sum(jnp.where(live_slot, route_weights.astype(jnp.float32), 0.0), axis=1)
    member = (live_expert[:, None] == jnp.arange(devices)[None, :]) & has_live[:, None]
    earlier = (jnp.arange(token_count)[None, :] < jnp.arange(token_count)[:, None]).astype(
        jnp.bfloat16
    )
    before = jnp.dot(earlier, member.astype(jnp.bfloat16), preferred_element_type=jnp.float32)
    slot_rank = jnp.sum(jnp.where(member, before, 0.0), axis=1)
    placed = member.T[:, None, :] & (
        slot_rank[None, None, :] == jnp.arange(CAP)[None, :, None].astype(jnp.float32)
    )
    dispatch_mat = placed.reshape(devices * CAP, token_count).astype(jnp.bfloat16)
    model_cols = model_width
    pad_cols = 128
    rows_send = (
        jnp.dot(dispatch_mat, moe_input, preferred_element_type=jnp.float32)
        .astype(jnp.bfloat16)
        .reshape(devices, CAP, model_width)
    )
    grads_send = (
        jnp.dot(dispatch_mat, out_grad, preferred_element_type=jnp.float32)
        .astype(jnp.bfloat16)
        .reshape(devices, CAP, model_width)
    )
    weights_send = jnp.sum(jnp.where(placed, token_weight[None, None, :], 0.0), axis=2).astype(
        jnp.bfloat16
    )
    send_all = jnp.concatenate(
        [
            rows_send,
            grads_send,
            jnp.broadcast_to(weights_send[:, :, None], (devices, CAP, pad_cols)),
        ],
        axis=2,
    )
    hidden_cols = gate_proj.shape[2]
    weight_cat = jnp.concatenate(
        [gate_proj, up_proj, jnp.transpose(down_proj, (0, 2, 1))], axis=2
    )
    gathered, weight_cat = lax.optimization_barrier((gathered, weight_cat))
    weight_full = lax.all_gather(weight_cat, "dp", axis=1, tiled=True)[0]
    gate_mat = weight_full[:, :hidden_cols]
    up_mat = weight_full[:, hidden_cols : 2 * hidden_cols]
    down_mat = jnp.transpose(weight_full[:, 2 * hidden_cols :])
    recv_all = lax.all_to_all(send_all, "expert", split_axis=0, concat_axis=0, tiled=True)
    rows_in = recv_all[:, :, :model_cols]
    grads_in = recv_all[:, :, model_cols : 2 * model_cols]
    weights_in = recv_all[:, :, 2 * model_cols]
    flat_rows = rows_in.reshape(devices * CAP, model_width)
    flat_grads = grads_in.reshape(devices * CAP, model_width)
    gate_pre = jnp.dot(flat_rows, gate_mat, preferred_element_type=jnp.float32)
    up_pre = jnp.dot(flat_rows, up_mat, preferred_element_type=jnp.float32)
    sigmoid_pre = jax.nn.sigmoid(gate_pre)
    silu_value = gate_pre * sigmoid_pre
    hidden = (silu_value * up_pre).astype(jnp.bfloat16)
    expert_out = jnp.dot(hidden, down_mat, preferred_element_type=jnp.float32)
    weight_back = jnp.sum(expert_out * flat_grads.astype(jnp.float32), axis=1).astype(jnp.bfloat16)
    scaled_grad = (
        weights_in.reshape(-1)[:, None].astype(jnp.float32) * flat_grads.astype(jnp.float32)
    ).astype(jnp.bfloat16)
    contract_last = (((1,), (1,)), ((), ()))
    hidden_grad = lax.dot_general(
        scaled_grad, down_mat, contract_last, preferred_element_type=jnp.float32
    )
    slope = sigmoid_pre * (1.0 + gate_pre * (1.0 - sigmoid_pre))
    gate_rows = (hidden_grad * up_pre * slope).astype(jnp.bfloat16)
    up_rows = (hidden_grad * silu_value).astype(jnp.bfloat16)
    input_rows = (
        lax.dot_general(gate_rows, gate_mat, contract_last, preferred_element_type=jnp.float32)
        + lax.dot_general(up_rows, up_mat, contract_last, preferred_element_type=jnp.float32)
    ).astype(jnp.bfloat16)
    hidden_width = hidden.shape[1]
    contract_first = (((0,), (0,)), ((), ()))
    summed = lax.psum_scatter(
        jnp.concatenate(
            [
                lax.dot_general(
                    flat_rows, gate_rows, contract_first, preferred_element_type=jnp.float32
                ),
                lax.dot_general(
                    flat_rows, up_rows, contract_first, preferred_element_type=jnp.float32
                ),
                lax.dot_general(
                    scaled_grad, hidden, contract_first, preferred_element_type=jnp.float32
                ),
            ],
            axis=1,
        ).astype(jnp.bfloat16),
        "dp",
        scatter_dimension=0,
        tiled=True,
    ).astype(jnp.float32)
    gate_proj_grad = summed[:, :hidden_width][None]
    up_proj_grad = summed[:, hidden_width : 2 * hidden_width][None]
    down_proj_grad = jnp.transpose(summed[:, 2 * hidden_width :])[None]
    pair_total = pair_return(pair_buffer)
    key_grad = pair_total[:, :, :HEAD]
    value_grad = pair_total[:, :, HEAD:]
    back_all = lax.all_to_all(
        jnp.concatenate(
            [
                input_rows.reshape(devices, CAP, model_width),
                jnp.broadcast_to(weight_back.reshape(devices, CAP, 1), (devices, CAP, pad_cols)),
            ],
            axis=2,
        ),
        "expert",
        split_axis=0,
        concat_axis=0,
        tiled=True,
    )
    input_back = back_all[:, :, :model_width]
    weights_back = back_all[:, :, model_width]
    input_grad = lax.dot_general(
        dispatch_mat,
        input_back.reshape(devices * CAP, model_width),
        contract_first,
        preferred_element_type=jnp.float32,
    ).astype(jnp.bfloat16)
    token_back = jnp.sum(
        dispatch_mat.astype(jnp.float32) * weights_back.reshape(-1).astype(jnp.float32)[:, None],
        axis=0,
    )
    route_grad = jnp.where(live_slot, token_back[:, None], 0.0).astype(jnp.bfloat16)
    return (
        query_grad,
        key_grad,
        value_grad,
        gate_grad,
        input_grad,
        route_grad,
        gate_proj_grad,
        up_proj_grad,
        down_proj_grad,
    )


def solution(mesh):
    return jax.shard_map(
        shards,
        mesh=mesh,
        in_specs=(
            P("dp", "expert", None),
            P("dp", "expert", None),
            P("dp", "expert", None),
            P("dp", "expert", None),
            P("dp", "expert", None),
            P(("dp", "expert"), None),
            P(("dp", "expert"), None),
            P(("dp", "expert"), None),
            P(("dp", "expert"), None),
            P("expert", "dp", None),
            P("expert", "dp", None),
            P("expert", None, "dp"),
        ),
        out_specs=(
            P("dp", "expert", None),
            P("dp", "expert", None),
            P("dp", "expert", None),
            P("dp", "expert", None),
            P(("dp", "expert"), None),
            P(("dp", "expert"), None),
            P("expert", "dp", None),
            P("expert", "dp", None),
            P("expert", None, "dp"),
        ),
        check_vma=False,
    )
```

```python
import jax
import jax.numpy as jnp
from jax import lax
from jax.experimental import pallas as pl
from jax.experimental.pallas import tpu as pltpu
from jax.sharding import PartitionSpec as P

HEADS = 8
HEAD = 256
CAP = 2
CHAIN_DTYPE = jnp.bfloat16


def pair_chain_kernel(parts_ref, out_ref, sendbuf, recvbuf, send_sems, recv_sems):
    devices, seqs = parts_ref.shape[0], parts_ref.shape[1]
    me = lax.axis_index("expert")
    row = lax.axis_index("dp")
    mesh_ids = pl.DeviceIdType.MESH
    has_upper = me < devices - 1
    is_top = me == devices - 1
    upper = lax.rem(me + 1, devices)
    lower = lax.rem(me + devices - 1, devices)

    def link(block, seq, peer):
        return pltpu.make_async_remote_copy(
            src_ref=sendbuf.at[block, seq],
            dst_ref=recvbuf.at[block, seq],
            send_sem=send_sems.at[block, seq],
            recv_sem=recv_sems.at[block, seq],
            device_id=(row, peer),
            device_id_type=mesh_ids,
        )

    barrier = pltpu.get_barrier_semaphore()
    for peer in (upper, lower):
        pl.semaphore_signal(barrier, inc=1, device_id=(row, peer), device_id_type=mesh_ids)
    pl.semaphore_wait(barrier, 2)

    for seq in range(seqs):

        @pl.when(has_upper)
        def _():
            link(me, seq, upper).wait_recv()
            out_ref[seq] = (
                parts_ref[me, seq].astype(jnp.float32) + recvbuf[me, seq].astype(jnp.float32)
            ).astype(out_ref.dtype)

        @pl.when(is_top)
        def _():
            out_ref[seq] = parts_ref[me, seq]

    def forward(step, carry):
        block = me - 1 - step
        for seq in range(seqs):

            @pl.when(has_upper)
            def _():
                link(block, seq, upper).wait_recv()
                sendbuf[block, seq] = (
                    parts_ref[block, seq].astype(jnp.float32)
                    + recvbuf[block, seq].astype(jnp.float32)
                ).astype(sendbuf.dtype)

            @pl.when(is_top)
            def _():
                sendbuf[block, seq] = parts_ref[block, seq].astype(sendbuf.dtype)

            link(block, seq, lower).start()
        return carry

    lax.fori_loop(0, me, forward, 0)

    def finish(step, carry):
        block = me - 1 - step
        for seq in range(seqs):
            link(block, seq, lower).wait_send()
        return carry

    lax.fori_loop(0, me, finish, 0)


def pair_return(pair_buffer):
    return pl.pallas_call(
        pair_chain_kernel,
        out_shape=jax.ShapeDtypeStruct(pair_buffer.shape[1:], pair_buffer.dtype),
        in_specs=[pl.BlockSpec(memory_space=pltpu.VMEM)],
        out_specs=pl.BlockSpec(memory_space=pltpu.VMEM),
        scratch_shapes=[
            pltpu.VMEM(pair_buffer.shape, CHAIN_DTYPE),
            pltpu.VMEM(pair_buffer.shape, CHAIN_DTYPE),
            pltpu.SemaphoreType.DMA(pair_buffer.shape[:2]),
            pltpu.SemaphoreType.DMA(pair_buffer.shape[:2]),
        ],
        compiler_params=pltpu.CompilerParams(collective_id=0, has_side_effects=True),
    )(pair_buffer)


def shards(
    query_rows,
    key_rows,
    value_rows,
    gate_logits,
    gated_grad,
    moe_input,
    out_grad,
    routes,
    route_weights,
    gate_proj,
    up_proj,
    down_proj,
):
    seq_count, shard_len, row_width = query_rows.shape
    devices = lax.axis_size("expert")
    position = lax.axis_index("expert")
    first_position = position * shard_len
    last_position = first_position + shard_len - 1
    total_len = shard_len * devices
    score_scale = HEAD ** (-0.5)
    queries = query_rows.reshape(seq_count, shard_len, HEADS, HEAD)
    packed = jnp.concatenate([key_rows, value_rows], axis=2)
    gathered = lax.all_gather(packed, "expert", axis=1, tiled=True)

    token_count, model_width = moe_input.shape
    live_slot = routes < devices
    has_live = jnp.any(live_slot, axis=1)
    live_expert = jnp.sum(jnp.where(live_slot, routes, 0), axis=1)
    token_weight = jnp.sum(jnp.where(live_slot, route_weights.astype(jnp.float32), 0.0), axis=1)
    member = (live_expert[:, None] == jnp.arange(devices)[None, :]) & has_live[:, None]
    earlier = (jnp.arange(token_count)[None, :] < jnp.arange(token_count)[:, None]).astype(
        jnp.bfloat16
    )
    before = jnp.dot(earlier, member.astype(jnp.bfloat16), preferred_element_type=jnp.float32)
    slot_rank = jnp.sum(jnp.where(member, before, 0.0), axis=1)
    placed = member.T[:, None, :] & (
        slot_rank[None, None, :] == jnp.arange(CAP)[None, :, None].astype(jnp.float32)
    )
    dispatch_mat = placed.reshape(devices * CAP, token_count).astype(jnp.bfloat16)
    model_cols = model_width
    pad_cols = 128
    rows_send = (
        jnp.dot(dispatch_mat, moe_input, preferred_element_type=jnp.float32)
        .astype(jnp.bfloat16)
        .reshape(devices, CAP, model_width)
    )
    grads_send = (
        jnp.dot(dispatch_mat, out_grad, preferred_element_type=jnp.float32)
        .astype(jnp.bfloat16)
        .reshape(devices, CAP, model_width)
    )
    weights_send = jnp.sum(jnp.where(placed, token_weight[None, None, :], 0.0), axis=2).astype(
        jnp.bfloat16
    )
    send_all = jnp.concatenate(
        [
            rows_send,
            grads_send,
            jnp.broadcast_to(weights_send[:, :, None], (devices, CAP, pad_cols)),
        ],
        axis=2,
    )
    hidden_cols = gate_proj.shape[2]
    weight_cat = jnp.concatenate(
        [gate_proj, up_proj, jnp.transpose(down_proj, (0, 2, 1))], axis=2
    )
    recv_all = lax.all_to_all(send_all, "expert", split_axis=0, concat_axis=0, tiled=True)
    gathered, recv_all, weight_cat = lax.optimization_barrier((gathered, recv_all, weight_cat))
    rows_in = recv_all[:, :, :model_cols]
    grads_in = recv_all[:, :, model_cols : 2 * model_cols]
    weights_in = recv_all[:, :, 2 * model_cols]
    weight_full = lax.all_gather(weight_cat, "dp", axis=1, tiled=True)[0]
    gate_mat = weight_full[:, :hidden_cols]
    up_mat = weight_full[:, hidden_cols : 2 * hidden_cols]
    down_mat = jnp.transpose(weight_full[:, 2 * hidden_cols :])
    keys_all = gathered[:, :, :HEAD]
    values_all = gathered[:, :, HEAD:]
    scores = (
        jnp.einsum("sphd,srd->shpr", queries, keys_all, preferred_element_type=jnp.float32)
        * score_scale
    )
    query_pos = first_position + jnp.arange(shard_len)
    key_pos = jnp.arange(total_len)
    allowed = (key_pos[None, :] <= query_pos[:, None])[None, None]
    masked = jnp.where(allowed, scores, -jnp.inf)
    row_max = jnp.max(masked, axis=3, keepdims=True)
    log_total = row_max + jnp.log(jnp.sum(jnp.exp(masked - row_max), axis=3, keepdims=True))
    exact_probs = jnp.where(allowed, jnp.exp(scores - log_total), 0.0)
    probs_low = exact_probs.astype(jnp.bfloat16)
    context = jnp.einsum(
        "shpr,srd->sphd", probs_low, values_all, preferred_element_type=jnp.float32
    )
    sigmoid_gate = jax.nn.sigmoid(gate_logits.astype(jnp.float32)).reshape(
        seq_count, shard_len, HEADS, HEAD
    )
    upstream = gated_grad.astype(jnp.float32).reshape(seq_count, shard_len, HEADS, HEAD)
    context_grad = (upstream * sigmoid_gate).astype(jnp.bfloat16)
    gate_grad = (
        (upstream * context * sigmoid_gate * (1.0 - sigmoid_gate))
        .astype(jnp.bfloat16)
        .reshape(seq_count, shard_len, row_width)
    )
    grad_dot = jnp.transpose(jnp.sum(context_grad.astype(jnp.float32) * context, axis=3), (0, 2, 1))
    prob_grad = jnp.einsum(
        "sphd,srd->shpr", context_grad, values_all, preferred_element_type=jnp.float32
    )
    score_grad = (exact_probs * (prob_grad - grad_dot[..., None]) * score_scale).astype(
        jnp.bfloat16
    )
    query_total = jnp.einsum(
        "shpr,srd->sphd", score_grad, keys_all, preferred_element_type=jnp.float32
    )
    key_part = jnp.einsum(
        "shpr,sphd->srd", score_grad, queries, preferred_element_type=jnp.float32
    ).astype(jnp.bfloat16)
    value_part = jnp.einsum(
        "shpr,sphd->srd", probs_low, context_grad, preferred_element_type=jnp.float32
    ).astype(jnp.bfloat16)
    pair_buffer = (
        jnp.moveaxis(
            jnp.concatenate([key_part, value_part], axis=2).reshape(
                seq_count, devices, shard_len, 2 * HEAD
            ),
            1,
            0,
        )
    )
    query_grad = query_total.astype(jnp.bfloat16).reshape(seq_count, shard_len, row_width)
    flat_rows = rows_in.reshape(devices * CAP, model_width)
    flat_grads = grads_in.reshape(devices * CAP, model_width)
    gate_pre = jnp.dot(flat_rows, gate_mat, preferred_element_type=jnp.float32)
    up_pre = jnp.dot(flat_rows, up_mat, preferred_element_type=jnp.float32)
    sigmoid_pre = jax.nn.sigmoid(gate_pre)
    silu_value = gate_pre * sigmoid_pre
    hidden = (silu_value * up_pre).astype(jnp.bfloat16)
    expert_out = jnp.dot(hidden, down_mat, preferred_element_type=jnp.float32)
    weight_back = jnp.sum(expert_out * flat_grads.astype(jnp.float32), axis=1).astype(jnp.bfloat16)
    scaled_grad = (
        weights_in.reshape(-1)[:, None].astype(jnp.float32) * flat_grads.astype(jnp.float32)
    ).astype(jnp.bfloat16)
    contract_last = (((1,), (1,)), ((), ()))
    hidden_grad = lax.dot_general(
        scaled_grad, down_mat, contract_last, preferred_element_type=jnp.float32
    )
    slope = sigmoid_pre * (1.0 + gate_pre * (1.0 - sigmoid_pre))
    gate_rows = (hidden_grad * up_pre * slope).astype(jnp.bfloat16)
    up_rows = (hidden_grad * silu_value).astype(jnp.bfloat16)
    input_rows = (
        lax.dot_general(gate_rows, gate_mat, contract_last, preferred_element_type=jnp.float32)
        + lax.dot_general(up_rows, up_mat, contract_last, preferred_element_type=jnp.float32)
    ).astype(jnp.bfloat16)
    hidden_width = hidden.shape[1]
    contract_first = (((0,), (0,)), ((), ()))
    summed = lax.psum_scatter(
        jnp.concatenate(
            [
                lax.dot_general(
                    flat_rows, gate_rows, contract_first, preferred_element_type=jnp.float32
                ),
                lax.dot_general(
                    flat_rows, up_rows, contract_first, preferred_element_type=jnp.float32
                ),
                lax.dot_general(
                    scaled_grad, hidden, contract_first, preferred_element_type=jnp.float32
                ),
            ],
            axis=1,
        ).astype(jnp.bfloat16),
        "dp",
        scatter_dimension=0,
        tiled=True,
    ).astype(jnp.float32)
    gate_proj_grad = summed[:, :hidden_width][None]
    up_proj_grad = summed[:, hidden_width : 2 * hidden_width][None]
    down_proj_grad = jnp.transpose(summed[:, 2 * hidden_width :])[None]
    pair_total = pair_return(pair_buffer)
    key_grad = pair_total[:, :, :HEAD]
    value_grad = pair_total[:, :, HEAD:]
    back_all = lax.all_to_all(
        jnp.concatenate(
            [
                input_rows.reshape(devices, CAP, model_width),
                jnp.broadcast_to(weight_back.reshape(devices, CAP, 1), (devices, CAP, pad_cols)),
            ],
            axis=2,
        ),
        "expert",
        split_axis=0,
        concat_axis=0,
        tiled=True,
    )
    input_back = back_all[:, :, :model_width]
    weights_back = back_all[:, :, model_width]
    input_grad = lax.dot_general(
        dispatch_mat,
        input_back.reshape(devices * CAP, model_width),
        contract_first,
        preferred_element_type=jnp.float32,
    ).astype(jnp.bfloat16)
    token_back = jnp.sum(
        dispatch_mat.astype(jnp.float32) * weights_back.reshape(-1).astype(jnp.float32)[:, None],
        axis=0,
    )
    route_grad = jnp.where(live_slot, token_back[:, None], 0.0).astype(jnp.bfloat16)
    return (
        query_grad,
        key_grad,
        value_grad,
        gate_grad,
        input_grad,
        route_grad,
        gate_proj_grad,
        up_proj_grad,
        down_proj_grad,
    )


def solution(mesh):
    return jax.shard_map(
        shards,
        mesh=mesh,
        in_specs=(
            P("dp", "expert", None),
            P("dp", "expert", None),
            P("dp", "expert", None),
            P("dp", "expert", None),
            P("dp", "expert", None),
            P(("dp", "expert"), None),
            P(("dp", "expert"), None),
            P(("dp", "expert"), None),
            P(("dp", "expert"), None),
            P("expert", "dp", None),
            P("expert", "dp", None),
            P("expert", None, "dp"),
        ),
        out_specs=(
            P("dp", "expert", None),
            P("dp", "expert", None),
            P("dp", "expert", None),
            P("dp", "expert", None),
            P(("dp", "expert"), None),
            P(("dp", "expert"), None),
            P("expert", "dp", None),
            P("expert", "dp", None),
            P("expert", None, "dp"),
        ),
        check_vma=False,
    )
```

```python
import jax
import jax.numpy as jnp
from jax import lax
from jax.experimental import pallas as pl
from jax.experimental.pallas import tpu as pltpu
from jax.sharding import PartitionSpec as P

HEADS = 8
HEAD = 256
CAP = 2
CHAIN_DTYPE = jnp.bfloat16


def pair_chain_kernel(parts_ref, out_ref, sendbuf, recvbuf, send_sems, recv_sems):
    devices, seqs = parts_ref.shape[0], parts_ref.shape[1]
    me = lax.axis_index("expert")
    row = lax.axis_index("dp")
    mesh_ids = pl.DeviceIdType.MESH
    has_upper = me < devices - 1
    is_top = me == devices - 1
    upper = lax.rem(me + 1, devices)
    lower = lax.rem(me + devices - 1, devices)

    def link(block, seq, peer):
        return pltpu.make_async_remote_copy(
            src_ref=sendbuf.at[block, seq],
            dst_ref=recvbuf.at[block, seq],
            send_sem=send_sems.at[block, seq],
            recv_sem=recv_sems.at[block, seq],
            device_id=(row, peer),
            device_id_type=mesh_ids,
        )

    barrier = pltpu.get_barrier_semaphore()
    for peer in (upper, lower):
        pl.semaphore_signal(barrier, inc=1, device_id=(row, peer), device_id_type=mesh_ids)
    pl.semaphore_wait(barrier, 2)

    for seq in range(seqs):

        @pl.when(has_upper)
        def _():
            link(me, seq, upper).wait_recv()
            out_ref[seq] = (
                parts_ref[me, seq].astype(jnp.float32) + recvbuf[me, seq].astype(jnp.float32)
            ).astype(out_ref.dtype)

        @pl.when(is_top)
        def _():
            out_ref[seq] = parts_ref[me, seq]

    def forward(step, carry):
        block = me - 1 - step
        for seq in range(seqs):

            @pl.when(has_upper)
            def _():
                link(block, seq, upper).wait_recv()
                sendbuf[block, seq] = (
                    parts_ref[block, seq].astype(jnp.float32)
                    + recvbuf[block, seq].astype(jnp.float32)
                ).astype(sendbuf.dtype)

            @pl.when(is_top)
            def _():
                sendbuf[block, seq] = parts_ref[block, seq].astype(sendbuf.dtype)

            link(block, seq, lower).start()
        return carry

    lax.fori_loop(0, me, forward, 0)

    def finish(step, carry):
        block = me - 1 - step
        for seq in range(seqs):
            link(block, seq, lower).wait_send()
        return carry

    lax.fori_loop(0, me, finish, 0)


def pair_return(pair_buffer):
    return pl.pallas_call(
        pair_chain_kernel,
        out_shape=jax.ShapeDtypeStruct(pair_buffer.shape[1:], pair_buffer.dtype),
        in_specs=[pl.BlockSpec(memory_space=pltpu.VMEM)],
        out_specs=pl.BlockSpec(memory_space=pltpu.VMEM),
        scratch_shapes=[
            pltpu.VMEM(pair_buffer.shape, CHAIN_DTYPE),
            pltpu.VMEM(pair_buffer.shape, CHAIN_DTYPE),
            pltpu.SemaphoreType.DMA(pair_buffer.shape[:2]),
            pltpu.SemaphoreType.DMA(pair_buffer.shape[:2]),
        ],
        compiler_params=pltpu.CompilerParams(collective_id=0, has_side_effects=True),
    )(pair_buffer)


def shards(
    query_rows,
    key_rows,
    value_rows,
    gate_logits,
    gated_grad,
    moe_input,
    out_grad,
    routes,
    route_weights,
    gate_proj,
    up_proj,
    down_proj,
):
    seq_count, shard_len, row_width = query_rows.shape
    devices = lax.axis_size("expert")
    position = lax.axis_index("expert")
    first_position = position * shard_len
    last_position = first_position + shard_len - 1
    total_len = shard_len * devices
    score_scale = HEAD ** (-0.5)
    queries = query_rows.reshape(seq_count, shard_len, HEADS, HEAD)
    packed = jnp.concatenate([key_rows, value_rows], axis=2)
    gathered = lax.all_gather(packed, "expert", axis=1, tiled=True)

    token_count, model_width = moe_input.shape
    live_slot = routes < devices
    has_live = jnp.any(live_slot, axis=1)
    live_expert = jnp.sum(jnp.where(live_slot, routes, 0), axis=1)
    token_weight = jnp.sum(jnp.where(live_slot, route_weights.astype(jnp.float32), 0.0), axis=1)
    member = (live_expert[:, None] == jnp.arange(devices)[None, :]) & has_live[:, None]
    earlier = (jnp.arange(token_count)[None, :] < jnp.arange(token_count)[:, None]).astype(
        jnp.bfloat16
    )
    before = jnp.dot(earlier, member.astype(jnp.bfloat16), preferred_element_type=jnp.float32)
    slot_rank = jnp.sum(jnp.where(member, before, 0.0), axis=1)
    placed = member.T[:, None, :] & (
        slot_rank[None, None, :] == jnp.arange(CAP)[None, :, None].astype(jnp.float32)
    )
    dispatch_mat = placed.reshape(devices * CAP, token_count).astype(jnp.bfloat16)
    model_cols = model_width
    pad_cols = 128
    rows_send = (
        jnp.dot(dispatch_mat, moe_input, preferred_element_type=jnp.float32)
        .astype(jnp.bfloat16)
        .reshape(devices, CAP, model_width)
    )
    grads_send = (
        jnp.dot(dispatch_mat, out_grad, preferred_element_type=jnp.float32)
        .astype(jnp.bfloat16)
        .reshape(devices, CAP, model_width)
    )
    weights_send = jnp.sum(jnp.where(placed, token_weight[None, None, :], 0.0), axis=2).astype(
        jnp.bfloat16
    )
    send_all = jnp.concatenate(
        [
            rows_send,
            grads_send,
            jnp.broadcast_to(weights_send[:, :, None], (devices, CAP, pad_cols)),
        ],
        axis=2,
    )
    hidden_cols = gate_proj.shape[2]
    weight_cat = jnp.concatenate(
        [gate_proj, up_proj, jnp.transpose(down_proj, (0, 2, 1))], axis=2
    )
    recv_all = lax.all_to_all(send_all, "expert", split_axis=0, concat_axis=0, tiled=True)
    gathered, recv_all, weight_cat = lax.optimization_barrier((gathered, recv_all, weight_cat))
    rows_in = recv_all[:, :, :model_cols]
    grads_in = recv_all[:, :, model_cols : 2 * model_cols]
    weights_in = recv_all[:, :, 2 * model_cols]
    weight_full = lax.all_gather(weight_cat, "dp", axis=1, tiled=True)[0]
    gate_mat = weight_full[:, :hidden_cols]
    up_mat = weight_full[:, hidden_cols : 2 * hidden_cols]
    down_mat = jnp.transpose(weight_full[:, 2 * hidden_cols :])
    keys_all = gathered[:, :, :HEAD]
    values_all = gathered[:, :, HEAD:]
    scores = (
        jnp.einsum("sphd,srd->shpr", queries, keys_all, preferred_element_type=jnp.float32)
        * score_scale
    )
    query_pos = first_position + jnp.arange(shard_len)
    key_pos = jnp.arange(total_len)
    allowed = (key_pos[None, :] <= query_pos[:, None])[None, None]
    masked = jnp.where(allowed, scores, -jnp.inf)
    row_max = jnp.max(masked, axis=3, keepdims=True)
    log_total = row_max + jnp.log(jnp.sum(jnp.exp(masked - row_max), axis=3, keepdims=True))
    exact_probs = jnp.where(allowed, jnp.exp(scores - log_total), 0.0)
    probs_low = exact_probs.astype(jnp.bfloat16)
    context = jnp.einsum(
        "shpr,srd->sphd", probs_low, values_all, preferred_element_type=jnp.float32
    )
    sigmoid_gate = jax.nn.sigmoid(gate_logits.astype(jnp.float32)).reshape(
        seq_count, shard_len, HEADS, HEAD
    )
    upstream = gated_grad.astype(jnp.float32).reshape(seq_count, shard_len, HEADS, HEAD)
    context_grad = (upstream * sigmoid_gate).astype(jnp.bfloat16)
    gate_grad = (
        (upstream * context * sigmoid_gate * (1.0 - sigmoid_gate))
        .astype(jnp.bfloat16)
        .reshape(seq_count, shard_len, row_width)
    )
    grad_dot = jnp.transpose(jnp.sum(context_grad.astype(jnp.float32) * context, axis=3), (0, 2, 1))
    prob_grad = jnp.einsum(
        "sphd,srd->shpr", context_grad, values_all, preferred_element_type=jnp.float32
    )
    score_grad = (exact_probs * (prob_grad - grad_dot[..., None]) * score_scale).astype(
        jnp.bfloat16
    )
    query_total = jnp.einsum(
        "shpr,srd->sphd", score_grad, keys_all, preferred_element_type=jnp.float32
    )
    key_part = jnp.einsum(
        "shpr,sphd->srd", score_grad, queries, preferred_element_type=jnp.float32
    ).astype(jnp.bfloat16)
    value_part = jnp.einsum(
        "shpr,sphd->srd", probs_low, context_grad, preferred_element_type=jnp.float32
    ).astype(jnp.bfloat16)
    pair_buffer = (
        jnp.moveaxis(
            jnp.concatenate([key_part, value_part], axis=2).reshape(
                seq_count, devices, shard_len, 2 * HEAD
            ),
            1,
            0,
        )
    )
    query_grad = query_total.astype(jnp.bfloat16).reshape(seq_count, shard_len, row_width)
    flat_rows = rows_in.reshape(devices * CAP, model_width)
    flat_grads = grads_in.reshape(devices * CAP, model_width)
    gate_pre = jnp.dot(flat_rows, gate_mat, preferred_element_type=jnp.float32)
    up_pre = jnp.dot(flat_rows, up_mat, preferred_element_type=jnp.float32)
    sigmoid_pre = jax.nn.sigmoid(gate_pre)
    silu_value = gate_pre * sigmoid_pre
    hidden = (silu_value * up_pre).astype(jnp.bfloat16)
    expert_out = jnp.dot(hidden, down_mat, preferred_element_type=jnp.float32)
    weight_back = jnp.sum(expert_out * flat_grads.astype(jnp.float32), axis=1).astype(jnp.bfloat16)
    scaled_grad = (
        weights_in.reshape(-1)[:, None].astype(jnp.float32) * flat_grads.astype(jnp.float32)
    ).astype(jnp.bfloat16)
    contract_last = (((1,), (1,)), ((), ()))
    hidden_grad = lax.dot_general(
        scaled_grad, down_mat, contract_last, preferred_element_type=jnp.float32
    )
    slope = sigmoid_pre * (1.0 + gate_pre * (1.0 - sigmoid_pre))
    gate_rows = (hidden_grad * up_pre * slope).astype(jnp.bfloat16)
    up_rows = (hidden_grad * silu_value).astype(jnp.bfloat16)
    input_rows = (
        lax.dot_general(gate_rows, gate_mat, contract_last, preferred_element_type=jnp.float32)
        + lax.dot_general(up_rows, up_mat, contract_last, preferred_element_type=jnp.float32)
    ).astype(jnp.bfloat16)
    hidden_width = hidden.shape[1]
    contract_first = (((0,), (0,)), ((), ()))
    summed = lax.psum_scatter(
        jnp.concatenate(
            [
                lax.dot_general(
                    flat_rows, gate_rows, contract_first, preferred_element_type=jnp.float32
                ),
                lax.dot_general(
                    flat_rows, up_rows, contract_first, preferred_element_type=jnp.float32
                ),
                lax.dot_general(
                    scaled_grad, hidden, contract_first, preferred_element_type=jnp.float32
                ),
            ],
            axis=1,
        ).astype(jnp.bfloat16),
        "dp",
        scatter_dimension=0,
        tiled=True,
    ).astype(jnp.float32)
    gate_proj_grad = summed[:, :hidden_width][None]
    up_proj_grad = summed[:, hidden_width : 2 * hidden_width][None]
    down_proj_grad = jnp.transpose(summed[:, 2 * hidden_width :])[None]
    chunks = 4
    pair_total = pair_return(
        pair_buffer.reshape(devices, chunks, seq_count * shard_len // chunks, 2 * HEAD)
    ).reshape(seq_count, shard_len, 2 * HEAD)
    key_grad = pair_total[:, :, :HEAD]
    value_grad = pair_total[:, :, HEAD:]
    back_all = lax.all_to_all(
        jnp.concatenate(
            [
                input_rows.reshape(devices, CAP, model_width),
                jnp.broadcast_to(weight_back.reshape(devices, CAP, 1), (devices, CAP, pad_cols)),
            ],
            axis=2,
        ),
        "expert",
        split_axis=0,
        concat_axis=0,
        tiled=True,
    )
    input_back = back_all[:, :, :model_width]
    weights_back = back_all[:, :, model_width]
    input_grad = lax.dot_general(
        dispatch_mat,
        input_back.reshape(devices * CAP, model_width),
        contract_first,
        preferred_element_type=jnp.float32,
    ).astype(jnp.bfloat16)
    token_back = jnp.sum(
        dispatch_mat.astype(jnp.float32) * weights_back.reshape(-1).astype(jnp.float32)[:, None],
        axis=0,
    )
    route_grad = jnp.where(live_slot, token_back[:, None], 0.0).astype(jnp.bfloat16)
    return (
        query_grad,
        key_grad,
        value_grad,
        gate_grad,
        input_grad,
        route_grad,
        gate_proj_grad,
        up_proj_grad,
        down_proj_grad,
    )


def solution(mesh):
    return jax.shard_map(
        shards,
        mesh=mesh,
        in_specs=(
            P("dp", "expert", None),
            P("dp", "expert", None),
            P("dp", "expert", None),
            P("dp", "expert", None),
            P("dp", "expert", None),
            P(("dp", "expert"), None),
            P(("dp", "expert"), None),
            P(("dp", "expert"), None),
            P(("dp", "expert"), None),
            P("expert", "dp", None),
            P("expert", "dp", None),
            P("expert", None, "dp"),
        ),
        out_specs=(
            P("dp", "expert", None),
            P("dp", "expert", None),
            P("dp", "expert", None),
            P("dp", "expert", None),
            P(("dp", "expert"), None),
            P(("dp", "expert"), None),
            P("expert", "dp", None),
            P("expert", "dp", None),
            P("expert", None, "dp"),
        ),
        check_vma=False,
    )
```

```python
import jax
import jax.numpy as jnp
from jax import lax
from jax.experimental import pallas as pl
from jax.experimental.pallas import tpu as pltpu
from jax.sharding import PartitionSpec as P

HEADS = 8
HEAD = 256
CAP = 2
CHAIN_DTYPE = jnp.bfloat16


def pair_chain_kernel(parts_ref, out_ref, sendbuf, recvbuf, send_sems, recv_sems):
    devices, seqs = parts_ref.shape[0], parts_ref.shape[1]
    me = lax.axis_index("expert")
    row = lax.axis_index("dp")
    mesh_ids = pl.DeviceIdType.MESH
    has_upper = me < devices - 1
    is_top = me == devices - 1
    upper = lax.rem(me + 1, devices)
    lower = lax.rem(me + devices - 1, devices)

    def link(block, seq, peer):
        return pltpu.make_async_remote_copy(
            src_ref=sendbuf.at[block, seq],
            dst_ref=recvbuf.at[block, seq],
            send_sem=send_sems.at[block, seq],
            recv_sem=recv_sems.at[block, seq],
            device_id=(row, peer),
            device_id_type=mesh_ids,
        )

    barrier = pltpu.get_barrier_semaphore()
    for peer in (upper, lower):
        pl.semaphore_signal(barrier, inc=1, device_id=(row, peer), device_id_type=mesh_ids)
    pl.semaphore_wait(barrier, 2)

    for seq in range(seqs):

        @pl.when(has_upper)
        def _():
            link(me, seq, upper).wait_recv()
            out_ref[seq] = (
                parts_ref[me, seq].astype(jnp.float32) + recvbuf[me, seq].astype(jnp.float32)
            ).astype(out_ref.dtype)

        @pl.when(is_top)
        def _():
            out_ref[seq] = parts_ref[me, seq]

    def forward(step, carry):
        block = me - 1 - step
        for seq in range(seqs):

            @pl.when(has_upper)
            def _():
                link(block, seq, upper).wait_recv()
                sendbuf[block, seq] = (
                    parts_ref[block, seq].astype(jnp.float32)
                    + recvbuf[block, seq].astype(jnp.float32)
                ).astype(sendbuf.dtype)

            @pl.when(is_top)
            def _():
                sendbuf[block, seq] = parts_ref[block, seq].astype(sendbuf.dtype)

            link(block, seq, lower).start()
        return carry

    lax.fori_loop(0, me, forward, 0)

    def finish(step, carry):
        block = me - 1 - step
        for seq in range(seqs):
            link(block, seq, lower).wait_send()
        return carry

    lax.fori_loop(0, me, finish, 0)


def pair_return(pair_buffer):
    return pl.pallas_call(
        pair_chain_kernel,
        out_shape=jax.ShapeDtypeStruct(pair_buffer.shape[1:], pair_buffer.dtype),
        in_specs=[pl.BlockSpec(memory_space=pltpu.VMEM)],
        out_specs=pl.BlockSpec(memory_space=pltpu.VMEM),
        scratch_shapes=[
            pltpu.VMEM(pair_buffer.shape, CHAIN_DTYPE),
            pltpu.VMEM(pair_buffer.shape, CHAIN_DTYPE),
            pltpu.SemaphoreType.DMA(pair_buffer.shape[:2]),
            pltpu.SemaphoreType.DMA(pair_buffer.shape[:2]),
        ],
        compiler_params=pltpu.CompilerParams(collective_id=0, has_side_effects=True),
    )(pair_buffer)


def shards(
    query_rows,
    key_rows,
    value_rows,
    gate_logits,
    gated_grad,
    moe_input,
    out_grad,
    routes,
    route_weights,
    gate_proj,
    up_proj,
    down_proj,
):
    seq_count, shard_len, row_width = query_rows.shape
    devices = lax.axis_size("expert")
    position = lax.axis_index("expert")
    first_position = position * shard_len
    last_position = first_position + shard_len - 1
    total_len = shard_len * devices
    score_scale = HEAD ** (-0.5)
    queries = query_rows.reshape(seq_count, shard_len, HEADS, HEAD)
    packed = jnp.concatenate([key_rows, value_rows], axis=2)

    token_count, model_width = moe_input.shape
    live_slot = routes < devices
    has_live = jnp.any(live_slot, axis=1)
    live_expert = jnp.sum(jnp.where(live_slot, routes, 0), axis=1)
    token_weight = jnp.sum(jnp.where(live_slot, route_weights.astype(jnp.float32), 0.0), axis=1)
    member = (live_expert[:, None] == jnp.arange(devices)[None, :]) & has_live[:, None]
    earlier = (jnp.arange(token_count)[None, :] < jnp.arange(token_count)[:, None]).astype(
        jnp.bfloat16
    )
    before = jnp.dot(earlier, member.astype(jnp.bfloat16), preferred_element_type=jnp.float32)
    slot_rank = jnp.sum(jnp.where(member, before, 0.0), axis=1)
    placed = member.T[:, None, :] & (
        slot_rank[None, None, :] == jnp.arange(CAP)[None, :, None].astype(jnp.float32)
    )
    dispatch_mat = placed.reshape(devices * CAP, token_count).astype(jnp.bfloat16)
    model_cols = model_width
    pad_cols = 128
    rows_send = (
        jnp.dot(dispatch_mat, moe_input, preferred_element_type=jnp.float32)
        .astype(jnp.bfloat16)
        .reshape(devices, CAP, model_width)
    )
    grads_send = (
        jnp.dot(dispatch_mat, out_grad, preferred_element_type=jnp.float32)
        .astype(jnp.bfloat16)
        .reshape(devices, CAP, model_width)
    )
    weights_send = jnp.sum(jnp.where(placed, token_weight[None, None, :], 0.0), axis=2).astype(
        jnp.bfloat16
    )
    send_all = jnp.concatenate(
        [
            rows_send,
            grads_send,
            jnp.broadcast_to(weights_send[:, :, None], (devices, CAP, pad_cols)),
        ],
        axis=2,
    )
    hidden_cols = gate_proj.shape[2]
    weight_cat = jnp.concatenate(
        [gate_proj, up_proj, jnp.transpose(down_proj, (0, 2, 1))], axis=2
    )
    recv_all = lax.all_to_all(send_all, "expert", split_axis=0, concat_axis=0, tiled=True)
    weight_full = lax.all_gather(weight_cat, "dp", axis=1, tiled=True)[0]
    packed, recv_all = lax.optimization_barrier((packed, recv_all))
    gathered = lax.all_gather(packed, "expert", axis=1, tiled=True)
    rows_in = recv_all[:, :, :model_cols]
    grads_in = recv_all[:, :, model_cols : 2 * model_cols]
    weights_in = recv_all[:, :, 2 * model_cols]
    gate_mat = weight_full[:, :hidden_cols]
    up_mat = weight_full[:, hidden_cols : 2 * hidden_cols]
    down_mat = jnp.transpose(weight_full[:, 2 * hidden_cols :])
    keys_all = gathered[:, :, :HEAD]
    values_all = gathered[:, :, HEAD:]
    scores = (
        jnp.einsum("sphd,srd->shpr", queries, keys_all, preferred_element_type=jnp.float32)
        * score_scale
    )
    query_pos = first_position + jnp.arange(shard_len)
    key_pos = jnp.arange(total_len)
    allowed = (key_pos[None, :] <= query_pos[:, None])[None, None]
    masked = jnp.where(allowed, scores, -jnp.inf)
    row_max = jnp.max(masked, axis=3, keepdims=True)
    log_total = row_max + jnp.log(jnp.sum(jnp.exp(masked - row_max), axis=3, keepdims=True))
    exact_probs = jnp.where(allowed, jnp.exp(scores - log_total), 0.0)
    probs_low = exact_probs.astype(jnp.bfloat16)
    context = jnp.einsum(
        "shpr,srd->sphd", probs_low, values_all, preferred_element_type=jnp.float32
    )
    sigmoid_gate = jax.nn.sigmoid(gate_logits.astype(jnp.float32)).reshape(
        seq_count, shard_len, HEADS, HEAD
    )
    upstream = gated_grad.astype(jnp.float32).reshape(seq_count, shard_len, HEADS, HEAD)
    context_grad = (upstream * sigmoid_gate).astype(jnp.bfloat16)
    gate_grad = (
        (upstream * context * sigmoid_gate * (1.0 - sigmoid_gate))
        .astype(jnp.bfloat16)
        .reshape(seq_count, shard_len, row_width)
    )
    grad_dot = jnp.transpose(jnp.sum(context_grad.astype(jnp.float32) * context, axis=3), (0, 2, 1))
    prob_grad = jnp.einsum(
        "sphd,srd->shpr", context_grad, values_all, preferred_element_type=jnp.float32
    )
    score_grad = (exact_probs * (prob_grad - grad_dot[..., None]) * score_scale).astype(
        jnp.bfloat16
    )
    query_total = jnp.einsum(
        "shpr,srd->sphd", score_grad, keys_all, preferred_element_type=jnp.float32
    )
    key_part = jnp.einsum(
        "shpr,sphd->srd", score_grad, queries, preferred_element_type=jnp.float32
    ).astype(jnp.bfloat16)
    value_part = jnp.einsum(
        "shpr,sphd->srd", probs_low, context_grad, preferred_element_type=jnp.float32
    ).astype(jnp.bfloat16)
    pair_buffer = (
        jnp.moveaxis(
            jnp.concatenate([key_part, value_part], axis=2).reshape(
                seq_count, devices, shard_len, 2 * HEAD
            ),
            1,
            0,
        )
    )
    query_grad = query_total.astype(jnp.bfloat16).reshape(seq_count, shard_len, row_width)
    flat_rows = rows_in.reshape(devices * CAP, model_width)
    flat_grads = grads_in.reshape(devices * CAP, model_width)
    gate_pre = jnp.dot(flat_rows, gate_mat, preferred_element_type=jnp.float32)
    up_pre = jnp.dot(flat_rows, up_mat, preferred_element_type=jnp.float32)
    sigmoid_pre = jax.nn.sigmoid(gate_pre)
    silu_value = gate_pre * sigmoid_pre
    hidden = (silu_value * up_pre).astype(jnp.bfloat16)
    expert_out = jnp.dot(hidden, down_mat, preferred_element_type=jnp.float32)
    weight_back = jnp.sum(expert_out * flat_grads.astype(jnp.float32), axis=1).astype(jnp.bfloat16)
    scaled_grad = (
        weights_in.reshape(-1)[:, None].astype(jnp.float32) * flat_grads.astype(jnp.float32)
    ).astype(jnp.bfloat16)
    contract_last = (((1,), (1,)), ((), ()))
    hidden_grad = lax.dot_general(
        scaled_grad, down_mat, contract_last, preferred_element_type=jnp.float32
    )
    slope = sigmoid_pre * (1.0 + gate_pre * (1.0 - sigmoid_pre))
    gate_rows = (hidden_grad * up_pre * slope).astype(jnp.bfloat16)
    up_rows = (hidden_grad * silu_value).astype(jnp.bfloat16)
    input_rows = (
        lax.dot_general(gate_rows, gate_mat, contract_last, preferred_element_type=jnp.float32)
        + lax.dot_general(up_rows, up_mat, contract_last, preferred_element_type=jnp.float32)
    ).astype(jnp.bfloat16)
    hidden_width = hidden.shape[1]
    contract_first = (((0,), (0,)), ((), ()))
    group_cat = jnp.concatenate(
            [
                lax.dot_general(
                    flat_rows, gate_rows, contract_first, preferred_element_type=jnp.float32
                ),
                lax.dot_general(
                    flat_rows, up_rows, contract_first, preferred_element_type=jnp.float32
                ),
                lax.dot_general(
                    scaled_grad, hidden, contract_first, preferred_element_type=jnp.float32
                ),
            ],
            axis=1,
        ).astype(jnp.bfloat16)
    gathered, group_cat = lax.optimization_barrier((gathered, group_cat))
    summed = lax.psum_scatter(group_cat, "dp", scatter_dimension=0, tiled=True).astype(
        jnp.float32
    )
    gate_proj_grad = summed[:, :hidden_width][None]
    up_proj_grad = summed[:, hidden_width : 2 * hidden_width][None]
    down_proj_grad = jnp.transpose(summed[:, 2 * hidden_width :])[None]
    chunks = 4
    pair_total = pair_return(
        pair_buffer.reshape(devices, chunks, seq_count * shard_len // chunks, 2 * HEAD)
    ).reshape(seq_count, shard_len, 2 * HEAD)
    key_grad = pair_total[:, :, :HEAD]
    value_grad = pair_total[:, :, HEAD:]
    back_all = lax.all_to_all(
        jnp.concatenate(
            [
                input_rows.reshape(devices, CAP, model_width),
                jnp.broadcast_to(weight_back.reshape(devices, CAP, 1), (devices, CAP, pad_cols)),
            ],
            axis=2,
        ),
        "expert",
        split_axis=0,
        concat_axis=0,
        tiled=True,
    )
    input_back = back_all[:, :, :model_width]
    weights_back = back_all[:, :, model_width]
    input_grad = lax.dot_general(
        dispatch_mat,
        input_back.reshape(devices * CAP, model_width),
        contract_first,
        preferred_element_type=jnp.float32,
    ).astype(jnp.bfloat16)
    token_back = jnp.sum(
        dispatch_mat.astype(jnp.float32) * weights_back.reshape(-1).astype(jnp.float32)[:, None],
        axis=0,
    )
    route_grad = jnp.where(live_slot, token_back[:, None], 0.0).astype(jnp.bfloat16)
    return (
        query_grad,
        key_grad,
        value_grad,
        gate_grad,
        input_grad,
        route_grad,
        gate_proj_grad,
        up_proj_grad,
        down_proj_grad,
    )


def solution(mesh):
    return jax.shard_map(
        shards,
        mesh=mesh,
        in_specs=(
            P("dp", "expert", None),
            P("dp", "expert", None),
            P("dp", "expert", None),
            P("dp", "expert", None),
            P("dp", "expert", None),
            P(("dp", "expert"), None),
            P(("dp", "expert"), None),
            P(("dp", "expert"), None),
            P(("dp", "expert"), None),
            P("expert", "dp", None),
            P("expert", "dp", None),
            P("expert", None, "dp"),
        ),
        out_specs=(
            P("dp", "expert", None),
            P("dp", "expert", None),
            P("dp", "expert", None),
            P("dp", "expert", None),
            P(("dp", "expert"), None),
            P(("dp", "expert"), None),
            P("expert", "dp", None),
            P("expert", "dp", None),
            P("expert", None, "dp"),
        ),
        check_vma=False,
    )
```

```python
import jax
import jax.numpy as jnp
from jax import lax
from jax.experimental import pallas as pl
from jax.experimental.pallas import tpu as pltpu
from jax.sharding import PartitionSpec as P

HEADS = 8
HEAD = 256
CAP = 2
CHAIN_DTYPE = jnp.bfloat16


def pair_chain_kernel(parts_ref, out_ref, sendbuf, recvbuf, send_sems, recv_sems):
    devices, chunks, rows = sendbuf.shape[0], sendbuf.shape[1], sendbuf.shape[2]
    seqs = parts_ref.shape[0]
    pieces = chunks // seqs
    block_rows = rows * pieces
    me = lax.axis_index("expert")
    row = lax.axis_index("dp")
    mesh_ids = pl.DeviceIdType.MESH
    has_upper = me < devices - 1
    is_top = me == devices - 1
    upper = lax.rem(me + 1, devices)
    lower = lax.rem(me + devices - 1, devices)

    def link(block, chunk, peer):
        return pltpu.make_async_remote_copy(
            src_ref=sendbuf.at[block, chunk],
            dst_ref=recvbuf.at[block, chunk],
            send_sem=send_sems.at[block, chunk],
            recv_sem=recv_sems.at[block, chunk],
            device_id=(row, peer),
            device_id_type=mesh_ids,
        )

    def own_part(block, chunk):
        start = pl.multiple_of(block * block_rows + (chunk % pieces) * rows, rows)
        return parts_ref[chunk // pieces, pl.ds(start, rows), :]

    barrier = pltpu.get_barrier_semaphore()
    for peer in (upper, lower):
        pl.semaphore_signal(barrier, inc=1, device_id=(row, peer), device_id_type=mesh_ids)
    pl.semaphore_wait(barrier, 2)

    for chunk in range(chunks):
        seq, piece = chunk // pieces, chunk % pieces
        out_rows = slice(piece * rows, (piece + 1) * rows)

        @pl.when(has_upper)
        def _():
            link(me, chunk, upper).wait_recv()
            out_ref[seq, out_rows, :] = (
                own_part(me, chunk).astype(jnp.float32) + recvbuf[me, chunk].astype(jnp.float32)
            ).astype(out_ref.dtype)

        @pl.when(is_top)
        def _():
            out_ref[seq, out_rows, :] = own_part(me, chunk)

    def forward(step, carry):
        block = me - 1 - step
        for chunk in range(chunks):

            @pl.when(has_upper)
            def _():
                link(block, chunk, upper).wait_recv()
                sendbuf[block, chunk] = (
                    own_part(block, chunk).astype(jnp.float32)
                    + recvbuf[block, chunk].astype(jnp.float32)
                ).astype(sendbuf.dtype)

            @pl.when(is_top)
            def _():
                sendbuf[block, chunk] = own_part(block, chunk).astype(sendbuf.dtype)

            link(block, chunk, lower).start()
        return carry

    lax.fori_loop(0, me, forward, 0)

    def finish(step, carry):
        block = me - 1 - step
        for chunk in range(chunks):
            link(block, chunk, lower).wait_send()
        return carry

    lax.fori_loop(0, me, finish, 0)


def pair_return(pair_buffer, devices, pieces):
    seqs, total_rows, width = pair_buffer.shape
    block_rows = total_rows // devices
    chunks = seqs * pieces
    slots = (devices, chunks, block_rows // pieces, width)
    return pl.pallas_call(
        pair_chain_kernel,
        out_shape=jax.ShapeDtypeStruct((seqs, block_rows, width), pair_buffer.dtype),
        in_specs=[pl.BlockSpec(memory_space=pltpu.VMEM)],
        out_specs=pl.BlockSpec(memory_space=pltpu.VMEM),
        scratch_shapes=[
            pltpu.VMEM(slots, CHAIN_DTYPE),
            pltpu.VMEM(slots, CHAIN_DTYPE),
            pltpu.SemaphoreType.DMA(slots[:2]),
            pltpu.SemaphoreType.DMA(slots[:2]),
        ],
        compiler_params=pltpu.CompilerParams(collective_id=0, has_side_effects=True),
    )(pair_buffer)


def shards(
    query_rows,
    key_rows,
    value_rows,
    gate_logits,
    gated_grad,
    moe_input,
    out_grad,
    routes,
    route_weights,
    gate_proj,
    up_proj,
    down_proj,
):
    seq_count, shard_len, row_width = query_rows.shape
    devices = lax.axis_size("expert")
    position = lax.axis_index("expert")
    first_position = position * shard_len
    last_position = first_position + shard_len - 1
    total_len = shard_len * devices
    score_scale = HEAD ** (-0.5)
    queries = query_rows.reshape(seq_count, shard_len, HEADS, HEAD)
    packed = jnp.concatenate([key_rows, value_rows], axis=2)

    token_count, model_width = moe_input.shape
    live_slot = routes < devices
    has_live = jnp.any(live_slot, axis=1)
    live_expert = jnp.sum(jnp.where(live_slot, routes, 0), axis=1)
    token_weight = jnp.sum(jnp.where(live_slot, route_weights.astype(jnp.float32), 0.0), axis=1)
    member = (live_expert[:, None] == jnp.arange(devices)[None, :]) & has_live[:, None]
    earlier = (jnp.arange(token_count)[None, :] < jnp.arange(token_count)[:, None]).astype(
        jnp.bfloat16
    )
    before = jnp.dot(earlier, member.astype(jnp.bfloat16), preferred_element_type=jnp.float32)
    slot_rank = jnp.sum(jnp.where(member, before, 0.0), axis=1)
    placed = member.T[:, None, :] & (
        slot_rank[None, None, :] == jnp.arange(CAP)[None, :, None].astype(jnp.float32)
    )
    dispatch_mat = placed.reshape(devices * CAP, token_count).astype(jnp.bfloat16)
    model_cols = model_width
    pad_cols = 128
    rows_send = (
        jnp.dot(dispatch_mat, moe_input, preferred_element_type=jnp.float32)
        .astype(jnp.bfloat16)
        .reshape(devices, CAP, model_width)
    )
    grads_send = (
        jnp.dot(dispatch_mat, out_grad, preferred_element_type=jnp.float32)
        .astype(jnp.bfloat16)
        .reshape(devices, CAP, model_width)
    )
    weights_send = jnp.sum(jnp.where(placed, token_weight[None, None, :], 0.0), axis=2).astype(
        jnp.bfloat16
    )
    send_all = jnp.concatenate(
        [
            rows_send,
            grads_send,
            jnp.broadcast_to(weights_send[:, :, None], (devices, CAP, pad_cols)),
        ],
        axis=2,
    )
    hidden_cols = gate_proj.shape[2]
    weight_cat = jnp.concatenate(
        [gate_proj, up_proj, jnp.transpose(down_proj, (0, 2, 1))], axis=2
    )
    recv_all = lax.all_to_all(send_all, "expert", split_axis=0, concat_axis=0, tiled=True)
    weight_full = lax.all_gather(weight_cat, "dp", axis=1, tiled=True)[0]
    packed, recv_all = lax.optimization_barrier((packed, recv_all))
    gathered = lax.all_gather(packed, "expert", axis=1, tiled=True)
    rows_in = recv_all[:, :, :model_cols]
    grads_in = recv_all[:, :, model_cols : 2 * model_cols]
    weights_in = recv_all[:, :, 2 * model_cols]
    gate_mat = weight_full[:, :hidden_cols]
    up_mat = weight_full[:, hidden_cols : 2 * hidden_cols]
    down_mat = jnp.transpose(weight_full[:, 2 * hidden_cols :])
    keys_all = gathered[:, :, :HEAD]
    values_all = gathered[:, :, HEAD:]
    scores = (
        jnp.einsum("sphd,srd->shpr", queries, keys_all, preferred_element_type=jnp.float32)
        * score_scale
    )
    query_pos = first_position + jnp.arange(shard_len)
    key_pos = jnp.arange(total_len)
    allowed = (key_pos[None, :] <= query_pos[:, None])[None, None]
    masked = jnp.where(allowed, scores, -jnp.inf)
    row_max = jnp.max(masked, axis=3, keepdims=True)
    log_total = row_max + jnp.log(jnp.sum(jnp.exp(masked - row_max), axis=3, keepdims=True))
    exact_probs = jnp.where(allowed, jnp.exp(scores - log_total), 0.0)
    probs_low = exact_probs.astype(jnp.bfloat16)
    context = jnp.einsum(
        "shpr,srd->sphd", probs_low, values_all, preferred_element_type=jnp.float32
    )
    sigmoid_gate = jax.nn.sigmoid(gate_logits.astype(jnp.float32)).reshape(
        seq_count, shard_len, HEADS, HEAD
    )
    upstream = gated_grad.astype(jnp.float32).reshape(seq_count, shard_len, HEADS, HEAD)
    context_grad = (upstream * sigmoid_gate).astype(jnp.bfloat16)
    gate_grad = (
        (upstream * context * sigmoid_gate * (1.0 - sigmoid_gate))
        .astype(jnp.bfloat16)
        .reshape(seq_count, shard_len, row_width)
    )
    grad_dot = jnp.transpose(jnp.sum(context_grad.astype(jnp.float32) * context, axis=3), (0, 2, 1))
    prob_grad = jnp.einsum(
        "sphd,srd->shpr", context_grad, values_all, preferred_element_type=jnp.float32
    )
    score_grad = (exact_probs * (prob_grad - grad_dot[..., None]) * score_scale).astype(
        jnp.bfloat16
    )
    query_total = jnp.einsum(
        "shpr,srd->sphd", score_grad, keys_all, preferred_element_type=jnp.float32
    )
    key_part = jnp.einsum(
        "shpr,sphd->srd", score_grad, queries, preferred_element_type=jnp.float32
    ).astype(jnp.bfloat16)
    value_part = jnp.einsum(
        "shpr,sphd->srd", probs_low, context_grad, preferred_element_type=jnp.float32
    ).astype(jnp.bfloat16)
    pair_buffer = jnp.concatenate([key_part, value_part], axis=2)
    query_grad = query_total.astype(jnp.bfloat16).reshape(seq_count, shard_len, row_width)
    flat_rows = rows_in.reshape(devices * CAP, model_width)
    flat_grads = grads_in.reshape(devices * CAP, model_width)
    gate_pre = jnp.dot(flat_rows, gate_mat, preferred_element_type=jnp.float32)
    up_pre = jnp.dot(flat_rows, up_mat, preferred_element_type=jnp.float32)
    sigmoid_pre = jax.nn.sigmoid(gate_pre)
    silu_value = gate_pre * sigmoid_pre
    hidden = (silu_value * up_pre).astype(jnp.bfloat16)
    expert_out = jnp.dot(hidden, down_mat, preferred_element_type=jnp.float32)
    weight_back = jnp.sum(expert_out * flat_grads.astype(jnp.float32), axis=1).astype(jnp.bfloat16)
    scaled_grad = (
        weights_in.reshape(-1)[:, None].astype(jnp.float32) * flat_grads.astype(jnp.float32)
    ).astype(jnp.bfloat16)
    contract_last = (((1,), (1,)), ((), ()))
    hidden_grad = lax.dot_general(
        scaled_grad, down_mat, contract_last, preferred_element_type=jnp.float32
    )
    slope = sigmoid_pre * (1.0 + gate_pre * (1.0 - sigmoid_pre))
    gate_rows = (hidden_grad * up_pre * slope).astype(jnp.bfloat16)
    up_rows = (hidden_grad * silu_value).astype(jnp.bfloat16)
    input_rows = (
        lax.dot_general(gate_rows, gate_mat, contract_last, preferred_element_type=jnp.float32)
        + lax.dot_general(up_rows, up_mat, contract_last, preferred_element_type=jnp.float32)
    ).astype(jnp.bfloat16)
    hidden_width = hidden.shape[1]
    contract_first = (((0,), (0,)), ((), ()))
    group_cat = jnp.concatenate(
            [
                lax.dot_general(
                    flat_rows, gate_rows, contract_first, preferred_element_type=jnp.float32
                ),
                lax.dot_general(
                    flat_rows, up_rows, contract_first, preferred_element_type=jnp.float32
                ),
                lax.dot_general(
                    scaled_grad, hidden, contract_first, preferred_element_type=jnp.float32
                ),
            ],
            axis=1,
        ).astype(jnp.bfloat16)
    gathered, group_cat = lax.optimization_barrier((gathered, group_cat))
    summed = lax.psum_scatter(group_cat, "dp", scatter_dimension=0, tiled=True).astype(
        jnp.float32
    )
    gate_proj_grad = summed[:, :hidden_width][None]
    up_proj_grad = summed[:, hidden_width : 2 * hidden_width][None]
    down_proj_grad = jnp.transpose(summed[:, 2 * hidden_width :])[None]
    pair_total = pair_return(pair_buffer, devices, 2)
    key_grad = pair_total[:, :, :HEAD]
    value_grad = pair_total[:, :, HEAD:]
    back_all = lax.all_to_all(
        jnp.concatenate(
            [
                input_rows.reshape(devices, CAP, model_width),
                jnp.broadcast_to(weight_back.reshape(devices, CAP, 1), (devices, CAP, pad_cols)),
            ],
            axis=2,
        ),
        "expert",
        split_axis=0,
        concat_axis=0,
        tiled=True,
    )
    input_back = back_all[:, :, :model_width]
    weights_back = back_all[:, :, model_width]
    input_grad = lax.dot_general(
        dispatch_mat,
        input_back.reshape(devices * CAP, model_width),
        contract_first,
        preferred_element_type=jnp.float32,
    ).astype(jnp.bfloat16)
    token_back = jnp.sum(
        dispatch_mat.astype(jnp.float32) * weights_back.reshape(-1).astype(jnp.float32)[:, None],
        axis=0,
    )
    route_grad = jnp.where(live_slot, token_back[:, None], 0.0).astype(jnp.bfloat16)
    return (
        query_grad,
        key_grad,
        value_grad,
        gate_grad,
        input_grad,
        route_grad,
        gate_proj_grad,
        up_proj_grad,
        down_proj_grad,
    )


def solution(mesh):
    return jax.shard_map(
        shards,
        mesh=mesh,
        in_specs=(
            P("dp", "expert", None),
            P("dp", "expert", None),
            P("dp", "expert", None),
            P("dp", "expert", None),
            P("dp", "expert", None),
            P(("dp", "expert"), None),
            P(("dp", "expert"), None),
            P(("dp", "expert"), None),
            P(("dp", "expert"), None),
            P("expert", "dp", None),
            P("expert", "dp", None),
            P("expert", None, "dp"),
        ),
        out_specs=(
            P("dp", "expert", None),
            P("dp", "expert", None),
            P("dp", "expert", None),
            P("dp", "expert", None),
            P(("dp", "expert"), None),
            P(("dp", "expert"), None),
            P("expert", "dp", None),
            P("expert", "dp", None),
            P("expert", None, "dp"),
        ),
        check_vma=False,
    )
```

```python
import jax
import jax.numpy as jnp
from jax import lax
from jax.experimental import pallas as pl
from jax.experimental.pallas import tpu as pltpu
from jax.sharding import PartitionSpec as P

HEADS = 8
HEAD = 256
CAP = 2
CHAIN_DTYPE = jnp.bfloat16


def pair_chain_kernel(parts_ref, out_ref, sendbuf, recvbuf, send_sems, recv_sems):
    devices, chunks, rows = sendbuf.shape[0], sendbuf.shape[1], sendbuf.shape[2]
    seqs = parts_ref.shape[0]
    pieces = chunks // seqs
    block_rows = rows * pieces
    me = lax.axis_index("expert")
    row = lax.axis_index("dp")
    mesh_ids = pl.DeviceIdType.MESH
    has_upper = me < devices - 1
    is_top = me == devices - 1
    upper = lax.rem(me + 1, devices)
    lower = lax.rem(me + devices - 1, devices)

    def link(block, chunk, peer):
        return pltpu.make_async_remote_copy(
            src_ref=sendbuf.at[block, chunk],
            dst_ref=recvbuf.at[block, chunk],
            send_sem=send_sems.at[block, chunk],
            recv_sem=recv_sems.at[block, chunk],
            device_id=(row, peer),
            device_id_type=mesh_ids,
        )

    def own_part(block, chunk):
        start = pl.multiple_of(block * block_rows + (chunk % pieces) * rows, rows)
        return parts_ref[chunk // pieces, pl.ds(start, rows), :]

    barrier = pltpu.get_barrier_semaphore()
    for peer in (upper, lower):
        pl.semaphore_signal(barrier, inc=1, device_id=(row, peer), device_id_type=mesh_ids)
    pl.semaphore_wait(barrier, 2)

    for chunk in range(chunks):
        seq, piece = chunk // pieces, chunk % pieces
        out_rows = slice(piece * rows, (piece + 1) * rows)

        @pl.when(has_upper)
        def _():
            link(me, chunk, upper).wait_recv()
            out_ref[seq, out_rows, :] = (
                own_part(me, chunk).astype(jnp.float32) + recvbuf[me, chunk].astype(jnp.float32)
            ).astype(out_ref.dtype)

        @pl.when(is_top)
        def _():
            out_ref[seq, out_rows, :] = own_part(me, chunk)

    def forward(step, carry):
        block = me - 1 - step
        for chunk in range(chunks):

            @pl.when(has_upper)
            def _():
                link(block, chunk, upper).wait_recv()
                sendbuf[block, chunk] = (
                    own_part(block, chunk).astype(jnp.float32)
                    + recvbuf[block, chunk].astype(jnp.float32)
                ).astype(sendbuf.dtype)

            @pl.when(is_top)
            def _():
                sendbuf[block, chunk] = own_part(block, chunk).astype(sendbuf.dtype)

            link(block, chunk, lower).start()
        return carry

    lax.fori_loop(0, me, forward, 0)

    def finish(step, carry):
        block = me - 1 - step
        for chunk in range(chunks):
            link(block, chunk, lower).wait_send()
        return carry

    lax.fori_loop(0, me, finish, 0)


def pair_return(pair_buffer, devices, pieces):
    seqs, total_rows, width = pair_buffer.shape
    block_rows = total_rows // devices
    chunks = seqs * pieces
    slots = (devices, chunks, block_rows // pieces, width)
    return pl.pallas_call(
        pair_chain_kernel,
        out_shape=jax.ShapeDtypeStruct((seqs, block_rows, width), pair_buffer.dtype),
        in_specs=[pl.BlockSpec(memory_space=pltpu.VMEM)],
        out_specs=pl.BlockSpec(memory_space=pltpu.VMEM),
        scratch_shapes=[
            pltpu.VMEM(slots, CHAIN_DTYPE),
            pltpu.VMEM(slots, CHAIN_DTYPE),
            pltpu.SemaphoreType.DMA(slots[:2]),
            pltpu.SemaphoreType.DMA(slots[:2]),
        ],
        compiler_params=pltpu.CompilerParams(collective_id=0, has_side_effects=True),
    )(pair_buffer)


def shards(
    query_rows,
    key_rows,
    value_rows,
    gate_logits,
    gated_grad,
    moe_input,
    out_grad,
    routes,
    route_weights,
    gate_proj,
    up_proj,
    down_proj,
):
    seq_count, shard_len, row_width = query_rows.shape
    devices = lax.axis_size("expert")
    position = lax.axis_index("expert")
    first_position = position * shard_len
    last_position = first_position + shard_len - 1
    total_len = shard_len * devices
    score_scale = HEAD ** (-0.5)
    queries = query_rows.reshape(seq_count, shard_len, HEADS, HEAD)
    packed = jnp.concatenate([key_rows, value_rows], axis=2)

    token_count, model_width = moe_input.shape
    live_slot = routes < devices
    has_live = jnp.any(live_slot, axis=1)
    live_expert = jnp.sum(jnp.where(live_slot, routes, 0), axis=1)
    token_weight = jnp.sum(jnp.where(live_slot, route_weights.astype(jnp.float32), 0.0), axis=1)
    member = (live_expert[:, None] == jnp.arange(devices)[None, :]) & has_live[:, None]
    earlier = (jnp.arange(token_count)[None, :] < jnp.arange(token_count)[:, None]).astype(
        jnp.bfloat16
    )
    before = jnp.dot(earlier, member.astype(jnp.bfloat16), preferred_element_type=jnp.float32)
    slot_rank = jnp.sum(jnp.where(member, before, 0.0), axis=1)
    placed = member.T[:, None, :] & (
        slot_rank[None, None, :] == jnp.arange(CAP)[None, :, None].astype(jnp.float32)
    )
    dispatch_mat = placed.reshape(devices * CAP, token_count).astype(jnp.bfloat16)
    model_cols = model_width
    pad_cols = 128
    rows_send = (
        jnp.dot(dispatch_mat, moe_input, preferred_element_type=jnp.float32)
        .astype(jnp.bfloat16)
        .reshape(devices, CAP, model_width)
    )
    grads_send = (
        jnp.dot(dispatch_mat, out_grad, preferred_element_type=jnp.float32)
        .astype(jnp.bfloat16)
        .reshape(devices, CAP, model_width)
    )
    weights_send = jnp.sum(jnp.where(placed, token_weight[None, None, :], 0.0), axis=2).astype(
        jnp.bfloat16
    )
    send_all = jnp.concatenate(
        [
            rows_send,
            grads_send,
            jnp.broadcast_to(weights_send[:, :, None], (devices, CAP, pad_cols)),
        ],
        axis=2,
    )
    hidden_cols = gate_proj.shape[2]
    weight_cat = jnp.concatenate(
        [gate_proj, up_proj, jnp.transpose(down_proj, (0, 2, 1))], axis=2
    )
    recv_all = lax.all_to_all(send_all, "expert", split_axis=0, concat_axis=0, tiled=True)
    weight_full = lax.all_gather(weight_cat, "dp", axis=1, tiled=True)[0]
    packed, recv_all = lax.optimization_barrier((packed, recv_all))
    gathered = lax.all_gather(packed, "expert", axis=1, tiled=True)
    rows_in = recv_all[:, :, :model_cols]
    grads_in = recv_all[:, :, model_cols : 2 * model_cols]
    weights_in = recv_all[:, :, 2 * model_cols]
    gate_mat = weight_full[:, :hidden_cols]
    up_mat = weight_full[:, hidden_cols : 2 * hidden_cols]
    down_mat = jnp.transpose(weight_full[:, 2 * hidden_cols :])
    keys_all = gathered[:, :, :HEAD]
    values_all = gathered[:, :, HEAD:]
    scores = (
        jnp.einsum("sphd,srd->shpr", queries, keys_all, preferred_element_type=jnp.float32)
        * score_scale
    )
    query_pos = first_position + jnp.arange(shard_len)
    key_pos = jnp.arange(total_len)
    allowed = (key_pos[None, :] <= query_pos[:, None])[None, None]
    masked = jnp.where(allowed, scores, -jnp.inf)
    row_max = jnp.max(masked, axis=3, keepdims=True)
    log_total = row_max + jnp.log(jnp.sum(jnp.exp(masked - row_max), axis=3, keepdims=True))
    exact_probs = jnp.where(allowed, jnp.exp(scores - log_total), 0.0)
    probs_low = exact_probs.astype(jnp.bfloat16)
    context = jnp.einsum(
        "shpr,srd->sphd", probs_low, values_all, preferred_element_type=jnp.float32
    )
    sigmoid_gate = jax.nn.sigmoid(gate_logits.astype(jnp.float32)).reshape(
        seq_count, shard_len, HEADS, HEAD
    )
    upstream = gated_grad.astype(jnp.float32).reshape(seq_count, shard_len, HEADS, HEAD)
    context_grad = (upstream * sigmoid_gate).astype(jnp.bfloat16)
    gate_grad = (
        (upstream * context * sigmoid_gate * (1.0 - sigmoid_gate))
        .astype(jnp.bfloat16)
        .reshape(seq_count, shard_len, row_width)
    )
    grad_dot = jnp.transpose(jnp.sum(context_grad.astype(jnp.float32) * context, axis=3), (0, 2, 1))
    prob_grad = jnp.einsum(
        "sphd,srd->shpr", context_grad, values_all, preferred_element_type=jnp.float32
    )
    score_grad = (exact_probs * (prob_grad - grad_dot[..., None]) * score_scale).astype(
        jnp.bfloat16
    )
    query_total = jnp.einsum(
        "shpr,srd->sphd", score_grad, keys_all, preferred_element_type=jnp.float32
    )
    key_part = jnp.einsum(
        "shpr,sphd->srd", score_grad, queries, preferred_element_type=jnp.float32
    ).astype(jnp.bfloat16)
    value_part = jnp.einsum(
        "shpr,sphd->srd", probs_low, context_grad, preferred_element_type=jnp.float32
    ).astype(jnp.bfloat16)
    pair_buffer = jnp.concatenate([key_part, value_part], axis=2)
    query_grad = query_total.astype(jnp.bfloat16).reshape(seq_count, shard_len, row_width)
    flat_rows = rows_in.reshape(devices * CAP, model_width)
    flat_grads = grads_in.reshape(devices * CAP, model_width)
    gate_pre = jnp.dot(flat_rows, gate_mat, preferred_element_type=jnp.float32)
    up_pre = jnp.dot(flat_rows, up_mat, preferred_element_type=jnp.float32)
    sigmoid_pre = jax.nn.sigmoid(gate_pre)
    silu_value = gate_pre * sigmoid_pre
    hidden = (silu_value * up_pre).astype(jnp.bfloat16)
    expert_out = jnp.dot(hidden, down_mat, preferred_element_type=jnp.float32)
    weight_back = jnp.sum(expert_out * flat_grads.astype(jnp.float32), axis=1).astype(jnp.bfloat16)
    scaled_grad = (
        weights_in.reshape(-1)[:, None].astype(jnp.float32) * flat_grads.astype(jnp.float32)
    ).astype(jnp.bfloat16)
    contract_last = (((1,), (1,)), ((), ()))
    hidden_grad = lax.dot_general(
        scaled_grad, down_mat, contract_last, preferred_element_type=jnp.float32
    )
    slope = sigmoid_pre * (1.0 + gate_pre * (1.0 - sigmoid_pre))
    gate_rows = (hidden_grad * up_pre * slope).astype(jnp.bfloat16)
    up_rows = (hidden_grad * silu_value).astype(jnp.bfloat16)
    input_rows = (
        lax.dot_general(gate_rows, gate_mat, contract_last, preferred_element_type=jnp.float32)
        + lax.dot_general(up_rows, up_mat, contract_last, preferred_element_type=jnp.float32)
    ).astype(jnp.bfloat16)
    hidden_width = hidden.shape[1]
    contract_first = (((0,), (0,)), ((), ()))
    group_cat = jnp.concatenate(
            [
                lax.dot_general(
                    flat_rows, gate_rows, contract_first, preferred_element_type=jnp.float32
                ),
                lax.dot_general(
                    flat_rows, up_rows, contract_first, preferred_element_type=jnp.float32
                ),
                lax.dot_general(
                    scaled_grad, hidden, contract_first, preferred_element_type=jnp.float32
                ),
            ],
            axis=1,
        ).astype(jnp.bfloat16)
    gathered, group_cat = lax.optimization_barrier((gathered, group_cat))
    summed = lax.psum_scatter(group_cat, "dp", scatter_dimension=0, tiled=True).astype(
        jnp.float32
    )
    gate_proj_grad = summed[:, :hidden_width][None]
    up_proj_grad = summed[:, hidden_width : 2 * hidden_width][None]
    down_proj_grad = jnp.transpose(summed[:, 2 * hidden_width :])[None]
    pair_total = pair_return(pair_buffer, devices, 4)
    key_grad = pair_total[:, :, :HEAD]
    value_grad = pair_total[:, :, HEAD:]
    back_all = lax.all_to_all(
        jnp.concatenate(
            [
                input_rows.reshape(devices, CAP, model_width),
                jnp.broadcast_to(weight_back.reshape(devices, CAP, 1), (devices, CAP, pad_cols)),
            ],
            axis=2,
        ),
        "expert",
        split_axis=0,
        concat_axis=0,
        tiled=True,
    )
    input_back = back_all[:, :, :model_width]
    weights_back = back_all[:, :, model_width]
    input_grad = lax.dot_general(
        dispatch_mat,
        input_back.reshape(devices * CAP, model_width),
        contract_first,
        preferred_element_type=jnp.float32,
    ).astype(jnp.bfloat16)
    token_back = jnp.sum(
        dispatch_mat.astype(jnp.float32) * weights_back.reshape(-1).astype(jnp.float32)[:, None],
        axis=0,
    )
    route_grad = jnp.where(live_slot, token_back[:, None], 0.0).astype(jnp.bfloat16)
    return (
        query_grad,
        key_grad,
        value_grad,
        gate_grad,
        input_grad,
        route_grad,
        gate_proj_grad,
        up_proj_grad,
        down_proj_grad,
    )


def solution(mesh):
    return jax.shard_map(
        shards,
        mesh=mesh,
        in_specs=(
            P("dp", "expert", None),
            P("dp", "expert", None),
            P("dp", "expert", None),
            P("dp", "expert", None),
            P("dp", "expert", None),
            P(("dp", "expert"), None),
            P(("dp", "expert"), None),
            P(("dp", "expert"), None),
            P(("dp", "expert"), None),
            P("expert", "dp", None),
            P("expert", "dp", None),
            P("expert", None, "dp"),
        ),
        out_specs=(
            P("dp", "expert", None),
            P("dp", "expert", None),
            P("dp", "expert", None),
            P("dp", "expert", None),
            P(("dp", "expert"), None),
            P(("dp", "expert"), None),
            P("expert", "dp", None),
            P("expert", "dp", None),
            P("expert", None, "dp"),
        ),
        check_vma=False,
    )
```

```python
import jax
import jax.numpy as jnp
from jax import lax
from jax.experimental import pallas as pl
from jax.experimental.pallas import tpu as pltpu
from jax.sharding import PartitionSpec as P

HEADS = 8
HEAD = 256
CAP = 2
CHAIN_DTYPE = jnp.bfloat16


def pair_chain_kernel(parts_ref, out_ref, sendbuf, recvbuf, send_sems, recv_sems):
    devices, chunks, rows = sendbuf.shape[0], sendbuf.shape[1], sendbuf.shape[2]
    seqs = parts_ref.shape[0]
    pieces = chunks // seqs
    block_rows = rows * pieces
    me = lax.axis_index("expert")
    row = lax.axis_index("dp")
    mesh_ids = pl.DeviceIdType.MESH
    has_upper = me < devices - 1
    is_top = me == devices - 1
    upper = lax.rem(me + 1, devices)
    lower = lax.rem(me + devices - 1, devices)

    def link(block, chunk, peer):
        return pltpu.make_async_remote_copy(
            src_ref=sendbuf.at[block, chunk],
            dst_ref=recvbuf.at[block, chunk],
            send_sem=send_sems.at[block, chunk],
            recv_sem=recv_sems.at[block, chunk],
            device_id=(row, peer),
            device_id_type=mesh_ids,
        )

    def own_part(block, chunk):
        start = pl.multiple_of(block * block_rows + (chunk % pieces) * rows, rows)
        return parts_ref[chunk // pieces, pl.ds(start, rows), :]

    barrier = pltpu.get_barrier_semaphore()
    for peer in (upper, lower):
        pl.semaphore_signal(barrier, inc=1, device_id=(row, peer), device_id_type=mesh_ids)
    pl.semaphore_wait(barrier, 2)

    for chunk in range(chunks):
        seq, piece = chunk // pieces, chunk % pieces
        out_rows = slice(piece * rows, (piece + 1) * rows)

        @pl.when(has_upper)
        def _():
            link(me, chunk, upper).wait_recv()
            out_ref[seq, out_rows, :] = (
                own_part(me, chunk).astype(jnp.float32) + recvbuf[me, chunk].astype(jnp.float32)
            ).astype(out_ref.dtype)

        @pl.when(is_top)
        def _():
            out_ref[seq, out_rows, :] = own_part(me, chunk)

    def forward(step, carry):
        block = me - 1 - step
        for chunk in range(chunks):

            @pl.when(has_upper)
            def _():
                link(block, chunk, upper).wait_recv()
                sendbuf[block, chunk] = (
                    own_part(block, chunk).astype(jnp.float32)
                    + recvbuf[block, chunk].astype(jnp.float32)
                ).astype(sendbuf.dtype)

            @pl.when(is_top)
            def _():
                sendbuf[block, chunk] = own_part(block, chunk).astype(sendbuf.dtype)

            link(block, chunk, lower).start()
        return carry

    lax.fori_loop(0, me, forward, 0)

    def finish(step, carry):
        block = me - 1 - step
        for chunk in range(chunks):
            link(block, chunk, lower).wait_send()
        return carry

    lax.fori_loop(0, me, finish, 0)


def pair_return(pair_buffer, devices, pieces):
    seqs, total_rows, width = pair_buffer.shape
    block_rows = total_rows // devices
    chunks = seqs * pieces
    slots = (devices, chunks, block_rows // pieces, width)
    return pl.pallas_call(
        pair_chain_kernel,
        out_shape=jax.ShapeDtypeStruct((seqs, block_rows, width), pair_buffer.dtype),
        in_specs=[pl.BlockSpec(memory_space=pltpu.VMEM)],
        out_specs=pl.BlockSpec(memory_space=pltpu.VMEM),
        scratch_shapes=[
            pltpu.VMEM(slots, CHAIN_DTYPE),
            pltpu.VMEM(slots, CHAIN_DTYPE),
            pltpu.SemaphoreType.DMA(slots[:2]),
            pltpu.SemaphoreType.DMA(slots[:2]),
        ],
        compiler_params=pltpu.CompilerParams(collective_id=0, has_side_effects=True),
    )(pair_buffer)


def shards(
    query_rows,
    key_rows,
    value_rows,
    gate_logits,
    gated_grad,
    moe_input,
    out_grad,
    routes,
    route_weights,
    gate_proj,
    up_proj,
    down_proj,
):
    seq_count, shard_len, row_width = query_rows.shape
    devices = lax.axis_size("expert")
    position = lax.axis_index("expert")
    first_position = position * shard_len
    last_position = first_position + shard_len - 1
    total_len = shard_len * devices
    score_scale = HEAD ** (-0.5)
    queries = query_rows.reshape(seq_count, shard_len, HEADS, HEAD)
    packed = jnp.concatenate([key_rows, value_rows], axis=2)

    token_count, model_width = moe_input.shape
    live_slot = routes < devices
    has_live = jnp.any(live_slot, axis=1)
    live_expert = jnp.sum(jnp.where(live_slot, routes, 0), axis=1)
    token_weight = jnp.sum(jnp.where(live_slot, route_weights.astype(jnp.float32), 0.0), axis=1)
    member = (live_expert[:, None] == jnp.arange(devices)[None, :]) & has_live[:, None]
    earlier = (jnp.arange(token_count)[None, :] < jnp.arange(token_count)[:, None]).astype(
        jnp.bfloat16
    )
    before = jnp.dot(earlier, member.astype(jnp.bfloat16), preferred_element_type=jnp.float32)
    slot_rank = jnp.sum(jnp.where(member, before, 0.0), axis=1)
    placed = member.T[:, None, :] & (
        slot_rank[None, None, :] == jnp.arange(CAP)[None, :, None].astype(jnp.float32)
    )
    dispatch_mat = placed.reshape(devices * CAP, token_count).astype(jnp.bfloat16)
    model_cols = model_width
    pad_cols = 128
    rows_send = (
        jnp.dot(dispatch_mat, moe_input, preferred_element_type=jnp.float32)
        .astype(jnp.bfloat16)
        .reshape(devices, CAP, model_width)
    )
    grads_send = (
        jnp.dot(dispatch_mat, out_grad, preferred_element_type=jnp.float32)
        .astype(jnp.bfloat16)
        .reshape(devices, CAP, model_width)
    )
    weights_send = jnp.sum(jnp.where(placed, token_weight[None, None, :], 0.0), axis=2).astype(
        jnp.bfloat16
    )
    send_all = jnp.concatenate(
        [
            rows_send,
            grads_send,
            jnp.broadcast_to(weights_send[:, :, None], (devices, CAP, pad_cols)),
        ],
        axis=2,
    )
    hidden_cols = gate_proj.shape[2]
    weight_cat = jnp.concatenate(
        [gate_proj, up_proj, jnp.transpose(down_proj, (0, 2, 1))], axis=2
    )
    recv_all = lax.all_to_all(send_all, "expert", split_axis=0, concat_axis=0, tiled=True)
    gathered = lax.all_gather(packed, "expert", axis=1, tiled=True)
    gathered, recv_all, weight_cat = lax.optimization_barrier((gathered, recv_all, weight_cat))
    weight_full = lax.all_gather(weight_cat, "dp", axis=1, tiled=True)[0]
    rows_in = recv_all[:, :, :model_cols]
    grads_in = recv_all[:, :, model_cols : 2 * model_cols]
    weights_in = recv_all[:, :, 2 * model_cols]
    gate_mat = weight_full[:, :hidden_cols]
    up_mat = weight_full[:, hidden_cols : 2 * hidden_cols]
    down_mat = jnp.transpose(weight_full[:, 2 * hidden_cols :])
    keys_all = gathered[:, :, :HEAD]
    values_all = gathered[:, :, HEAD:]
    scores = (
        jnp.einsum("sphd,srd->shpr", queries, keys_all, preferred_element_type=jnp.float32)
        * score_scale
    )
    query_pos = first_position + jnp.arange(shard_len)
    key_pos = jnp.arange(total_len)
    allowed = (key_pos[None, :] <= query_pos[:, None])[None, None]
    masked = jnp.where(allowed, scores, -jnp.inf)
    row_max = jnp.max(masked, axis=3, keepdims=True)
    log_total = row_max + jnp.log(jnp.sum(jnp.exp(masked - row_max), axis=3, keepdims=True))
    exact_probs = jnp.where(allowed, jnp.exp(scores - log_total), 0.0)
    probs_low = exact_probs.astype(jnp.bfloat16)
    context = jnp.einsum(
        "shpr,srd->sphd", probs_low, values_all, preferred_element_type=jnp.float32
    )
    sigmoid_gate = jax.nn.sigmoid(gate_logits.astype(jnp.float32)).reshape(
        seq_count, shard_len, HEADS, HEAD
    )
    upstream = gated_grad.astype(jnp.float32).reshape(seq_count, shard_len, HEADS, HEAD)
    context_grad = (upstream * sigmoid_gate).astype(jnp.bfloat16)
    gate_grad = (
        (upstream * context * sigmoid_gate * (1.0 - sigmoid_gate))
        .astype(jnp.bfloat16)
        .reshape(seq_count, shard_len, row_width)
    )
    grad_dot = jnp.transpose(jnp.sum(context_grad.astype(jnp.float32) * context, axis=3), (0, 2, 1))
    prob_grad = jnp.einsum(
        "sphd,srd->shpr", context_grad, values_all, preferred_element_type=jnp.float32
    )
    score_grad = (exact_probs * (prob_grad - grad_dot[..., None]) * score_scale).astype(
        jnp.bfloat16
    )
    query_total = jnp.einsum(
        "shpr,srd->sphd", score_grad, keys_all, preferred_element_type=jnp.float32
    )
    key_part = jnp.einsum(
        "shpr,sphd->srd", score_grad, queries, preferred_element_type=jnp.float32
    ).astype(jnp.bfloat16)
    value_part = jnp.einsum(
        "shpr,sphd->srd", probs_low, context_grad, preferred_element_type=jnp.float32
    ).astype(jnp.bfloat16)
    pair_buffer = jnp.concatenate([key_part, value_part], axis=2)
    query_grad = query_total.astype(jnp.bfloat16).reshape(seq_count, shard_len, row_width)
    flat_rows = rows_in.reshape(devices * CAP, model_width)
    flat_grads = grads_in.reshape(devices * CAP, model_width)
    gate_pre = jnp.dot(flat_rows, gate_mat, preferred_element_type=jnp.float32)
    up_pre = jnp.dot(flat_rows, up_mat, preferred_element_type=jnp.float32)
    sigmoid_pre = jax.nn.sigmoid(gate_pre)
    silu_value = gate_pre * sigmoid_pre
    hidden = (silu_value * up_pre).astype(jnp.bfloat16)
    expert_out = jnp.dot(hidden, down_mat, preferred_element_type=jnp.float32)
    weight_back = jnp.sum(expert_out * flat_grads.astype(jnp.float32), axis=1).astype(jnp.bfloat16)
    scaled_grad = (
        weights_in.reshape(-1)[:, None].astype(jnp.float32) * flat_grads.astype(jnp.float32)
    ).astype(jnp.bfloat16)
    contract_last = (((1,), (1,)), ((), ()))
    hidden_grad = lax.dot_general(
        scaled_grad, down_mat, contract_last, preferred_element_type=jnp.float32
    )
    slope = sigmoid_pre * (1.0 + gate_pre * (1.0 - sigmoid_pre))
    gate_rows = (hidden_grad * up_pre * slope).astype(jnp.bfloat16)
    up_rows = (hidden_grad * silu_value).astype(jnp.bfloat16)
    input_rows = (
        lax.dot_general(gate_rows, gate_mat, contract_last, preferred_element_type=jnp.float32)
        + lax.dot_general(up_rows, up_mat, contract_last, preferred_element_type=jnp.float32)
    ).astype(jnp.bfloat16)
    hidden_width = hidden.shape[1]
    contract_first = (((0,), (0,)), ((), ()))
    group_cat = jnp.concatenate(
            [
                lax.dot_general(
                    flat_rows, gate_rows, contract_first, preferred_element_type=jnp.float32
                ),
                lax.dot_general(
                    flat_rows, up_rows, contract_first, preferred_element_type=jnp.float32
                ),
                lax.dot_general(
                    scaled_grad, hidden, contract_first, preferred_element_type=jnp.float32
                ),
            ],
            axis=1,
        ).astype(jnp.bfloat16)
    summed = lax.psum_scatter(group_cat, "dp", scatter_dimension=0, tiled=True).astype(
        jnp.float32
    )
    gate_proj_grad = summed[:, :hidden_width][None]
    up_proj_grad = summed[:, hidden_width : 2 * hidden_width][None]
    down_proj_grad = jnp.transpose(summed[:, 2 * hidden_width :])[None]
    pair_total = pair_return(pair_buffer, devices, 4)
    key_grad = pair_total[:, :, :HEAD]
    value_grad = pair_total[:, :, HEAD:]
    back_all = lax.all_to_all(
        jnp.concatenate(
            [
                input_rows.reshape(devices, CAP, model_width),
                jnp.broadcast_to(weight_back.reshape(devices, CAP, 1), (devices, CAP, pad_cols)),
            ],
            axis=2,
        ),
        "expert",
        split_axis=0,
        concat_axis=0,
        tiled=True,
    )
    input_back = back_all[:, :, :model_width]
    weights_back = back_all[:, :, model_width]
    input_grad = lax.dot_general(
        dispatch_mat,
        input_back.reshape(devices * CAP, model_width),
        contract_first,
        preferred_element_type=jnp.float32,
    ).astype(jnp.bfloat16)
    token_back = jnp.sum(
        dispatch_mat.astype(jnp.float32) * weights_back.reshape(-1).astype(jnp.float32)[:, None],
        axis=0,
    )
    route_grad = jnp.where(live_slot, token_back[:, None], 0.0).astype(jnp.bfloat16)
    return (
        query_grad,
        key_grad,
        value_grad,
        gate_grad,
        input_grad,
        route_grad,
        gate_proj_grad,
        up_proj_grad,
        down_proj_grad,
    )


def solution(mesh):
    return jax.shard_map(
        shards,
        mesh=mesh,
        in_specs=(
            P("dp", "expert", None),
            P("dp", "expert", None),
            P("dp", "expert", None),
            P("dp", "expert", None),
            P("dp", "expert", None),
            P(("dp", "expert"), None),
            P(("dp", "expert"), None),
            P(("dp", "expert"), None),
            P(("dp", "expert"), None),
            P("expert", "dp", None),
            P("expert", "dp", None),
            P("expert", None, "dp"),
        ),
        out_specs=(
            P("dp", "expert", None),
            P("dp", "expert", None),
            P("dp", "expert", None),
            P("dp", "expert", None),
            P(("dp", "expert"), None),
            P(("dp", "expert"), None),
            P("expert", "dp", None),
            P("expert", "dp", None),
            P("expert", None, "dp"),
        ),
        check_vma=False,
    )
```

```python
import jax
import jax.numpy as jnp
from jax import lax
from jax.experimental import pallas as pl
from jax.experimental.pallas import tpu as pltpu
from jax.sharding import PartitionSpec as P

HEADS = 8
HEAD = 256
CAP = 2
CHAIN_DTYPE = jnp.bfloat16


def pair_chain_kernel(parts_ref, out_ref, sendbuf, recvbuf, send_sems, recv_sems):
    devices, chunks, rows = sendbuf.shape[0], sendbuf.shape[1], sendbuf.shape[2]
    seqs = parts_ref.shape[0]
    pieces = chunks // seqs
    block_rows = rows * pieces
    me = lax.axis_index("expert")
    row = lax.axis_index("dp")
    mesh_ids = pl.DeviceIdType.MESH
    has_upper = me < devices - 1
    is_top = me == devices - 1
    upper = lax.rem(me + 1, devices)
    lower = lax.rem(me + devices - 1, devices)

    def link(block, chunk, peer):
        return pltpu.make_async_remote_copy(
            src_ref=sendbuf.at[block, chunk],
            dst_ref=recvbuf.at[block, chunk],
            send_sem=send_sems.at[block, chunk],
            recv_sem=recv_sems.at[block, chunk],
            device_id=(row, peer),
            device_id_type=mesh_ids,
        )

    def own_part(block, chunk):
        start = pl.multiple_of(block * block_rows + (chunk % pieces) * rows, rows)
        return parts_ref[chunk // pieces, pl.ds(start, rows), :]

    barrier = pltpu.get_barrier_semaphore()
    for peer in (upper, lower):
        pl.semaphore_signal(barrier, inc=1, device_id=(row, peer), device_id_type=mesh_ids)
    pl.semaphore_wait(barrier, 2)

    for chunk in range(chunks):
        seq, piece = chunk // pieces, chunk % pieces
        out_rows = slice(piece * rows, (piece + 1) * rows)

        @pl.when(has_upper)
        def _():
            link(me, chunk, upper).wait_recv()
            out_ref[seq, out_rows, :] = (
                own_part(me, chunk).astype(jnp.float32) + recvbuf[me, chunk].astype(jnp.float32)
            ).astype(out_ref.dtype)

        @pl.when(is_top)
        def _():
            out_ref[seq, out_rows, :] = own_part(me, chunk)

    def forward(step, carry):
        block = me - 1 - step
        for chunk in range(chunks):

            @pl.when(has_upper)
            def _():
                link(block, chunk, upper).wait_recv()
                sendbuf[block, chunk] = (
                    own_part(block, chunk).astype(jnp.float32)
                    + recvbuf[block, chunk].astype(jnp.float32)
                ).astype(sendbuf.dtype)

            @pl.when(is_top)
            def _():
                sendbuf[block, chunk] = own_part(block, chunk).astype(sendbuf.dtype)

            link(block, chunk, lower).start()
        return carry

    lax.fori_loop(0, me, forward, 0)

    def finish(step, carry):
        block = me - 1 - step
        for chunk in range(chunks):
            link(block, chunk, lower).wait_send()
        return carry

    lax.fori_loop(0, me, finish, 0)


def pair_return(pair_buffer, devices, pieces):
    seqs, total_rows, width = pair_buffer.shape
    block_rows = total_rows // devices
    chunks = seqs * pieces
    slots = (devices, chunks, block_rows // pieces, width)
    return pl.pallas_call(
        pair_chain_kernel,
        out_shape=jax.ShapeDtypeStruct((seqs, block_rows, width), pair_buffer.dtype),
        in_specs=[pl.BlockSpec(memory_space=pltpu.VMEM)],
        out_specs=pl.BlockSpec(memory_space=pltpu.VMEM),
        scratch_shapes=[
            pltpu.VMEM(slots, CHAIN_DTYPE),
            pltpu.VMEM(slots, CHAIN_DTYPE),
            pltpu.SemaphoreType.DMA(slots[:2]),
            pltpu.SemaphoreType.DMA(slots[:2]),
        ],
        compiler_params=pltpu.CompilerParams(collective_id=0, has_side_effects=True),
    )(pair_buffer)


def shards(
    query_rows,
    key_rows,
    value_rows,
    gate_logits,
    gated_grad,
    moe_input,
    out_grad,
    routes,
    route_weights,
    gate_proj,
    up_proj,
    down_proj,
):
    seq_count, shard_len, row_width = query_rows.shape
    devices = lax.axis_size("expert")
    position = lax.axis_index("expert")
    first_position = position * shard_len
    last_position = first_position + shard_len - 1
    total_len = shard_len * devices
    score_scale = HEAD ** (-0.5)
    queries = query_rows.reshape(seq_count, shard_len, HEADS, HEAD)
    packed = jnp.concatenate([key_rows, value_rows], axis=2)

    token_count, model_width = moe_input.shape
    live_slot = routes < devices
    has_live = jnp.any(live_slot, axis=1)
    live_expert = jnp.sum(jnp.where(live_slot, routes, 0), axis=1)
    token_weight = jnp.sum(jnp.where(live_slot, route_weights.astype(jnp.float32), 0.0), axis=1)
    member = (live_expert[:, None] == jnp.arange(devices)[None, :]) & has_live[:, None]
    earlier = (jnp.arange(token_count)[None, :] < jnp.arange(token_count)[:, None]).astype(
        jnp.bfloat16
    )
    before = jnp.dot(earlier, member.astype(jnp.bfloat16), preferred_element_type=jnp.float32)
    slot_rank = jnp.sum(jnp.where(member, before, 0.0), axis=1)
    placed = member.T[:, None, :] & (
        slot_rank[None, None, :] == jnp.arange(CAP)[None, :, None].astype(jnp.float32)
    )
    dispatch_mat = placed.reshape(devices * CAP, token_count).astype(jnp.bfloat16)
    model_cols = model_width
    pad_cols = 128
    rows_send = (
        jnp.dot(dispatch_mat, moe_input, preferred_element_type=jnp.float32)
        .astype(jnp.bfloat16)
        .reshape(devices, CAP, model_width)
    )
    grads_send = (
        jnp.dot(dispatch_mat, out_grad, preferred_element_type=jnp.float32)
        .astype(jnp.bfloat16)
        .reshape(devices, CAP, model_width)
    )
    weights_send = jnp.sum(jnp.where(placed, token_weight[None, None, :], 0.0), axis=2).astype(
        jnp.bfloat16
    )
    send_all = jnp.concatenate(
        [
            rows_send,
            grads_send,
            jnp.broadcast_to(weights_send[:, :, None], (devices, CAP, pad_cols)),
        ],
        axis=2,
    )
    hidden_cols = gate_proj.shape[2]
    weight_cat = jnp.concatenate(
        [gate_proj, up_proj, jnp.transpose(down_proj, (0, 2, 1))], axis=2
    )
    recv_all = lax.all_to_all(send_all, "expert", split_axis=0, concat_axis=0, tiled=True)
    groups = lax.axis_size("dp")
    weight_full = lax.all_to_all(
        jnp.broadcast_to(weight_cat, (groups,) + weight_cat.shape[1:]),
        "dp",
        split_axis=0,
        concat_axis=0,
        tiled=True,
    ).reshape(groups * weight_cat.shape[1], weight_cat.shape[2])
    gathered = lax.all_gather(packed, "expert", axis=1, tiled=True)
    rows_in = recv_all[:, :, :model_cols]
    grads_in = recv_all[:, :, model_cols : 2 * model_cols]
    weights_in = recv_all[:, :, 2 * model_cols]
    gate_mat = weight_full[:, :hidden_cols]
    up_mat = weight_full[:, hidden_cols : 2 * hidden_cols]
    down_mat = jnp.transpose(weight_full[:, 2 * hidden_cols :])
    keys_all = gathered[:, :, :HEAD]
    values_all = gathered[:, :, HEAD:]
    scores = (
        jnp.einsum("sphd,srd->shpr", queries, keys_all, preferred_element_type=jnp.float32)
        * score_scale
    )
    query_pos = first_position + jnp.arange(shard_len)
    key_pos = jnp.arange(total_len)
    allowed = (key_pos[None, :] <= query_pos[:, None])[None, None]
    masked = jnp.where(allowed, scores, -jnp.inf)
    row_max = jnp.max(masked, axis=3, keepdims=True)
    log_total = row_max + jnp.log(jnp.sum(jnp.exp(masked - row_max), axis=3, keepdims=True))
    exact_probs = jnp.where(allowed, jnp.exp(scores - log_total), 0.0)
    probs_low = exact_probs.astype(jnp.bfloat16)
    context = jnp.einsum(
        "shpr,srd->sphd", probs_low, values_all, preferred_element_type=jnp.float32
    )
    sigmoid_gate = jax.nn.sigmoid(gate_logits.astype(jnp.float32)).reshape(
        seq_count, shard_len, HEADS, HEAD
    )
    upstream = gated_grad.astype(jnp.float32).reshape(seq_count, shard_len, HEADS, HEAD)
    context_grad = (upstream * sigmoid_gate).astype(jnp.bfloat16)
    gate_grad = (
        (upstream * context * sigmoid_gate * (1.0 - sigmoid_gate))
        .astype(jnp.bfloat16)
        .reshape(seq_count, shard_len, row_width)
    )
    grad_dot = jnp.transpose(jnp.sum(context_grad.astype(jnp.float32) * context, axis=3), (0, 2, 1))
    prob_grad = jnp.einsum(
        "sphd,srd->shpr", context_grad, values_all, preferred_element_type=jnp.float32
    )
    score_grad = (exact_probs * (prob_grad - grad_dot[..., None]) * score_scale).astype(
        jnp.bfloat16
    )
    query_total = jnp.einsum(
        "shpr,srd->sphd", score_grad, keys_all, preferred_element_type=jnp.float32
    )
    key_part = jnp.einsum(
        "shpr,sphd->srd", score_grad, queries, preferred_element_type=jnp.float32
    ).astype(jnp.bfloat16)
    value_part = jnp.einsum(
        "shpr,sphd->srd", probs_low, context_grad, preferred_element_type=jnp.float32
    ).astype(jnp.bfloat16)
    pair_buffer = jnp.concatenate([key_part, value_part], axis=2)
    query_grad = query_total.astype(jnp.bfloat16).reshape(seq_count, shard_len, row_width)
    flat_rows = rows_in.reshape(devices * CAP, model_width)
    flat_grads = grads_in.reshape(devices * CAP, model_width)
    gate_pre = jnp.dot(flat_rows, gate_mat, preferred_element_type=jnp.float32)
    up_pre = jnp.dot(flat_rows, up_mat, preferred_element_type=jnp.float32)
    sigmoid_pre = jax.nn.sigmoid(gate_pre)
    silu_value = gate_pre * sigmoid_pre
    hidden = (silu_value * up_pre).astype(jnp.bfloat16)
    expert_out = jnp.dot(hidden, down_mat, preferred_element_type=jnp.float32)
    weight_back = jnp.sum(expert_out * flat_grads.astype(jnp.float32), axis=1).astype(jnp.bfloat16)
    scaled_grad = (
        weights_in.reshape(-1)[:, None].astype(jnp.float32) * flat_grads.astype(jnp.float32)
    ).astype(jnp.bfloat16)
    contract_last = (((1,), (1,)), ((), ()))
    hidden_grad = lax.dot_general(
        scaled_grad, down_mat, contract_last, preferred_element_type=jnp.float32
    )
    slope = sigmoid_pre * (1.0 + gate_pre * (1.0 - sigmoid_pre))
    gate_rows = (hidden_grad * up_pre * slope).astype(jnp.bfloat16)
    up_rows = (hidden_grad * silu_value).astype(jnp.bfloat16)
    input_rows = (
        lax.dot_general(gate_rows, gate_mat, contract_last, preferred_element_type=jnp.float32)
        + lax.dot_general(up_rows, up_mat, contract_last, preferred_element_type=jnp.float32)
    ).astype(jnp.bfloat16)
    hidden_width = hidden.shape[1]
    contract_first = (((0,), (0,)), ((), ()))
    group_cat = jnp.concatenate(
            [
                lax.dot_general(
                    flat_rows, gate_rows, contract_first, preferred_element_type=jnp.float32
                ),
                lax.dot_general(
                    flat_rows, up_rows, contract_first, preferred_element_type=jnp.float32
                ),
                lax.dot_general(
                    scaled_grad, hidden, contract_first, preferred_element_type=jnp.float32
                ),
            ],
            axis=1,
        ).astype(jnp.bfloat16)
    gathered, group_cat = lax.optimization_barrier((gathered, group_cat))
    summed = lax.psum_scatter(group_cat, "dp", scatter_dimension=0, tiled=True).astype(
        jnp.float32
    )
    gate_proj_grad = summed[:, :hidden_width][None]
    up_proj_grad = summed[:, hidden_width : 2 * hidden_width][None]
    down_proj_grad = jnp.transpose(summed[:, 2 * hidden_width :])[None]
    pair_total = pair_return(pair_buffer, devices, 4)
    key_grad = pair_total[:, :, :HEAD]
    value_grad = pair_total[:, :, HEAD:]
    back_all = lax.all_to_all(
        jnp.concatenate(
            [
                input_rows.reshape(devices, CAP, model_width),
                jnp.broadcast_to(weight_back.reshape(devices, CAP, 1), (devices, CAP, pad_cols)),
            ],
            axis=2,
        ),
        "expert",
        split_axis=0,
        concat_axis=0,
        tiled=True,
    )
    input_back = back_all[:, :, :model_width]
    weights_back = back_all[:, :, model_width]
    input_grad = lax.dot_general(
        dispatch_mat,
        input_back.reshape(devices * CAP, model_width),
        contract_first,
        preferred_element_type=jnp.float32,
    ).astype(jnp.bfloat16)
    token_back = jnp.sum(
        dispatch_mat.astype(jnp.float32) * weights_back.reshape(-1).astype(jnp.float32)[:, None],
        axis=0,
    )
    route_grad = jnp.where(live_slot, token_back[:, None], 0.0).astype(jnp.bfloat16)
    return (
        query_grad,
        key_grad,
        value_grad,
        gate_grad,
        input_grad,
        route_grad,
        gate_proj_grad,
        up_proj_grad,
        down_proj_grad,
    )


def solution(mesh):
    return jax.shard_map(
        shards,
        mesh=mesh,
        in_specs=(
            P("dp", "expert", None),
            P("dp", "expert", None),
            P("dp", "expert", None),
            P("dp", "expert", None),
            P("dp", "expert", None),
            P(("dp", "expert"), None),
            P(("dp", "expert"), None),
            P(("dp", "expert"), None),
            P(("dp", "expert"), None),
            P("expert", "dp", None),
            P("expert", "dp", None),
            P("expert", None, "dp"),
        ),
        out_specs=(
            P("dp", "expert", None),
            P("dp", "expert", None),
            P("dp", "expert", None),
            P("dp", "expert", None),
            P(("dp", "expert"), None),
            P(("dp", "expert"), None),
            P("expert", "dp", None),
            P("expert", "dp", None),
            P("expert", None, "dp"),
        ),
        check_vma=False,
    )
```

```python
import jax
import jax.numpy as jnp
from jax import lax
from jax.experimental import pallas as pl
from jax.experimental.pallas import tpu as pltpu
from jax.sharding import PartitionSpec as P

HEADS = 8
HEAD = 256
CAP = 2
CHAIN_DTYPE = jnp.bfloat16


def pair_chain_kernel(parts_ref, out_ref, sendbuf, recvbuf, send_sems, recv_sems):
    devices, chunks, rows = sendbuf.shape[0], sendbuf.shape[1], sendbuf.shape[2]
    seqs = parts_ref.shape[0]
    pieces = chunks // seqs
    block_rows = rows * pieces
    me = lax.axis_index("expert")
    row = lax.axis_index("dp")
    mesh_ids = pl.DeviceIdType.MESH
    has_upper = me < devices - 1
    is_top = me == devices - 1
    upper = lax.rem(me + 1, devices)
    lower = lax.rem(me + devices - 1, devices)

    def link(block, chunk, peer):
        return pltpu.make_async_remote_copy(
            src_ref=sendbuf.at[block, chunk],
            dst_ref=recvbuf.at[block, chunk],
            send_sem=send_sems.at[block, chunk],
            recv_sem=recv_sems.at[block, chunk],
            device_id=(row, peer),
            device_id_type=mesh_ids,
        )

    def own_part(block, chunk):
        start = pl.multiple_of(block * block_rows + (chunk % pieces) * rows, rows)
        return parts_ref[chunk // pieces, pl.ds(start, rows), :]

    barrier = pltpu.get_barrier_semaphore()
    for peer in (upper, lower):
        pl.semaphore_signal(barrier, inc=1, device_id=(row, peer), device_id_type=mesh_ids)
    pl.semaphore_wait(barrier, 2)

    for chunk in range(chunks):
        seq, piece = chunk // pieces, chunk % pieces
        out_rows = slice(piece * rows, (piece + 1) * rows)

        @pl.when(has_upper)
        def _():
            link(me, chunk, upper).wait_recv()
            out_ref[seq, out_rows, :] = (
                own_part(me, chunk).astype(jnp.float32) + recvbuf[me, chunk].astype(jnp.float32)
            ).astype(out_ref.dtype)

        @pl.when(is_top)
        def _():
            out_ref[seq, out_rows, :] = own_part(me, chunk)

    def forward(step, carry):
        block = me - 1 - step
        for chunk in range(chunks):

            @pl.when(has_upper)
            def _():
                link(block, chunk, upper).wait_recv()
                sendbuf[block, chunk] = (
                    own_part(block, chunk).astype(jnp.float32)
                    + recvbuf[block, chunk].astype(jnp.float32)
                ).astype(sendbuf.dtype)

            @pl.when(is_top)
            def _():
                sendbuf[block, chunk] = own_part(block, chunk).astype(sendbuf.dtype)

            link(block, chunk, lower).start()
        return carry

    lax.fori_loop(0, me, forward, 0)

    def finish(step, carry):
        block = me - 1 - step
        for chunk in range(chunks):
            link(block, chunk, lower).wait_send()
        return carry

    lax.fori_loop(0, me, finish, 0)


def pair_return(pair_buffer, devices, pieces):
    seqs, total_rows, width = pair_buffer.shape
    block_rows = total_rows // devices
    chunks = seqs * pieces
    slots = (devices, chunks, block_rows // pieces, width)
    return pl.pallas_call(
        pair_chain_kernel,
        out_shape=jax.ShapeDtypeStruct((seqs, block_rows, width), pair_buffer.dtype),
        in_specs=[pl.BlockSpec(memory_space=pltpu.VMEM)],
        out_specs=pl.BlockSpec(memory_space=pltpu.VMEM),
        scratch_shapes=[
            pltpu.VMEM(slots, CHAIN_DTYPE),
            pltpu.VMEM(slots, CHAIN_DTYPE),
            pltpu.SemaphoreType.DMA(slots[:2]),
            pltpu.SemaphoreType.DMA(slots[:2]),
        ],
        compiler_params=pltpu.CompilerParams(collective_id=0, has_side_effects=True),
    )(pair_buffer)


def shards(
    query_rows,
    key_rows,
    value_rows,
    gate_logits,
    gated_grad,
    moe_input,
    out_grad,
    routes,
    route_weights,
    gate_proj,
    up_proj,
    down_proj,
):
    seq_count, shard_len, row_width = query_rows.shape
    devices = lax.axis_size("expert")
    position = lax.axis_index("expert")
    first_position = position * shard_len
    last_position = first_position + shard_len - 1
    total_len = shard_len * devices
    score_scale = HEAD ** (-0.5)
    queries = query_rows.reshape(seq_count, shard_len, HEADS, HEAD)
    packed = jnp.concatenate([key_rows, value_rows], axis=2)

    token_count, model_width = moe_input.shape
    live_slot = routes < devices
    has_live = jnp.any(live_slot, axis=1)
    live_expert = jnp.sum(jnp.where(live_slot, routes, 0), axis=1)
    token_weight = jnp.sum(jnp.where(live_slot, route_weights.astype(jnp.float32), 0.0), axis=1)
    member = (live_expert[:, None] == jnp.arange(devices)[None, :]) & has_live[:, None]
    earlier = (jnp.arange(token_count)[None, :] < jnp.arange(token_count)[:, None]).astype(
        jnp.bfloat16
    )
    before = jnp.dot(earlier, member.astype(jnp.bfloat16), preferred_element_type=jnp.float32)
    slot_rank = jnp.sum(jnp.where(member, before, 0.0), axis=1)
    placed = member.T[:, None, :] & (
        slot_rank[None, None, :] == jnp.arange(CAP)[None, :, None].astype(jnp.float32)
    )
    dispatch_mat = placed.reshape(devices * CAP, token_count).astype(jnp.bfloat16)
    model_cols = model_width
    pad_cols = 128
    rows_send = (
        jnp.dot(dispatch_mat, moe_input, preferred_element_type=jnp.float32)
        .astype(jnp.bfloat16)
        .reshape(devices, CAP, model_width)
    )
    grads_send = (
        jnp.dot(dispatch_mat, out_grad, preferred_element_type=jnp.float32)
        .astype(jnp.bfloat16)
        .reshape(devices, CAP, model_width)
    )
    weights_send = jnp.sum(jnp.where(placed, token_weight[None, None, :], 0.0), axis=2).astype(
        jnp.bfloat16
    )
    send_all = jnp.concatenate(
        [
            rows_send,
            grads_send,
            jnp.broadcast_to(weights_send[:, :, None], (devices, CAP, pad_cols)),
        ],
        axis=2,
    )
    hidden_cols = gate_proj.shape[2]
    weight_cat = jnp.concatenate(
        [gate_proj, up_proj, jnp.transpose(down_proj, (0, 2, 1))], axis=2
    )
    recv_all = lax.all_to_all(send_all, "expert", split_axis=0, concat_axis=0, tiled=True)
    groups = lax.axis_size("dp")
    weight_full = lax.all_to_all(
        jnp.broadcast_to(weight_cat, (groups,) + weight_cat.shape[1:]),
        "dp",
        split_axis=0,
        concat_axis=0,
        tiled=True,
    ).reshape(groups * weight_cat.shape[1], weight_cat.shape[2])
    gathered = lax.all_gather(packed, "expert", axis=1, tiled=True)
    rows_in = recv_all[:, :, :model_cols]
    grads_in = recv_all[:, :, model_cols : 2 * model_cols]
    weights_in = recv_all[:, :, 2 * model_cols]
    gate_mat = weight_full[:, :hidden_cols]
    up_mat = weight_full[:, hidden_cols : 2 * hidden_cols]
    down_mat = jnp.transpose(weight_full[:, 2 * hidden_cols :])
    keys_all = gathered[:, :, :HEAD]
    values_all = gathered[:, :, HEAD:]
    scores = (
        jnp.einsum("sphd,srd->shpr", queries, keys_all, preferred_element_type=jnp.float32)
        * score_scale
    )
    query_pos = first_position + jnp.arange(shard_len)
    key_pos = jnp.arange(total_len)
    allowed = (key_pos[None, :] <= query_pos[:, None])[None, None]
    masked = jnp.where(allowed, scores, -jnp.inf)
    row_max = jnp.max(masked, axis=3, keepdims=True)
    log_total = row_max + jnp.log(jnp.sum(jnp.exp(masked - row_max), axis=3, keepdims=True))
    exact_probs = jnp.where(allowed, jnp.exp(scores - log_total), 0.0)
    probs_low = exact_probs.astype(jnp.bfloat16)
    context = jnp.einsum(
        "shpr,srd->sphd", probs_low, values_all, preferred_element_type=jnp.float32
    )
    sigmoid_gate = jax.nn.sigmoid(gate_logits.astype(jnp.float32)).reshape(
        seq_count, shard_len, HEADS, HEAD
    )
    upstream = gated_grad.astype(jnp.float32).reshape(seq_count, shard_len, HEADS, HEAD)
    context_grad = (upstream * sigmoid_gate).astype(jnp.bfloat16)
    gate_grad = (
        (upstream * context * sigmoid_gate * (1.0 - sigmoid_gate))
        .astype(jnp.bfloat16)
        .reshape(seq_count, shard_len, row_width)
    )
    grad_dot = jnp.transpose(jnp.sum(context_grad.astype(jnp.float32) * context, axis=3), (0, 2, 1))
    prob_grad = jnp.einsum(
        "sphd,srd->shpr", context_grad, values_all, preferred_element_type=jnp.float32
    )
    score_grad = (exact_probs * (prob_grad - grad_dot[..., None]) * score_scale).astype(
        jnp.bfloat16
    )
    query_total = jnp.einsum(
        "shpr,srd->sphd", score_grad, keys_all, preferred_element_type=jnp.float32
    )
    key_part = jnp.einsum(
        "shpr,sphd->srd", score_grad, queries, preferred_element_type=jnp.float32
    ).astype(jnp.bfloat16)
    value_part = jnp.einsum(
        "shpr,sphd->srd", probs_low, context_grad, preferred_element_type=jnp.float32
    ).astype(jnp.bfloat16)
    pair_buffer = jnp.concatenate([key_part, value_part], axis=2)
    query_grad = query_total.astype(jnp.bfloat16).reshape(seq_count, shard_len, row_width)
    flat_rows = rows_in.reshape(devices * CAP, model_width)
    flat_grads = grads_in.reshape(devices * CAP, model_width)
    gate_pre = jnp.dot(flat_rows, gate_mat, preferred_element_type=jnp.float32)
    up_pre = jnp.dot(flat_rows, up_mat, preferred_element_type=jnp.float32)
    sigmoid_pre = jax.nn.sigmoid(gate_pre)
    silu_value = gate_pre * sigmoid_pre
    hidden = (silu_value * up_pre).astype(jnp.bfloat16)
    expert_out = jnp.dot(hidden, down_mat, preferred_element_type=jnp.float32)
    weight_back = jnp.sum(expert_out * flat_grads.astype(jnp.float32), axis=1).astype(jnp.bfloat16)
    scaled_grad = (
        weights_in.reshape(-1)[:, None].astype(jnp.float32) * flat_grads.astype(jnp.float32)
    ).astype(jnp.bfloat16)
    contract_last = (((1,), (1,)), ((), ()))
    hidden_grad = lax.dot_general(
        scaled_grad, down_mat, contract_last, preferred_element_type=jnp.float32
    )
    slope = sigmoid_pre * (1.0 + gate_pre * (1.0 - sigmoid_pre))
    gate_rows = (hidden_grad * up_pre * slope).astype(jnp.bfloat16)
    up_rows = (hidden_grad * silu_value).astype(jnp.bfloat16)
    input_rows = (
        lax.dot_general(gate_rows, gate_mat, contract_last, preferred_element_type=jnp.float32)
        + lax.dot_general(up_rows, up_mat, contract_last, preferred_element_type=jnp.float32)
    ).astype(jnp.bfloat16)
    hidden_width = hidden.shape[1]
    contract_first = (((0,), (0,)), ((), ()))
    group_cat = jnp.concatenate(
            [
                lax.dot_general(
                    flat_rows, gate_rows, contract_first, preferred_element_type=jnp.float32
                ),
                lax.dot_general(
                    flat_rows, up_rows, contract_first, preferred_element_type=jnp.float32
                ),
                lax.dot_general(
                    scaled_grad, hidden, contract_first, preferred_element_type=jnp.float32
                ),
            ],
            axis=1,
        ).astype(jnp.bfloat16)
    gathered, group_cat = lax.optimization_barrier((gathered, group_cat))
    summed = lax.psum_scatter(group_cat, "dp", scatter_dimension=0, tiled=True).astype(
        jnp.float32
    )
    gate_proj_grad = summed[:, :hidden_width][None]
    up_proj_grad = summed[:, hidden_width : 2 * hidden_width][None]
    down_proj_grad = jnp.transpose(summed[:, 2 * hidden_width :])[None]
    pair_total = pair_return(pair_buffer, devices, 4)
    key_grad = pair_total[:, :, :HEAD]
    value_grad = pair_total[:, :, HEAD:]
    back_send = jnp.concatenate(
            [
                input_rows.reshape(devices, CAP, model_width),
                jnp.broadcast_to(weight_back.reshape(devices, CAP, 1), (devices, CAP, pad_cols)),
            ],
            axis=2,
        )
    pair_total, back_send = lax.optimization_barrier((pair_total, back_send))
    back_all = lax.all_to_all(
        back_send,
        "expert",
        split_axis=0,
        concat_axis=0,
        tiled=True,
    )
    input_back = back_all[:, :, :model_width]
    weights_back = back_all[:, :, model_width]
    input_grad = lax.dot_general(
        dispatch_mat,
        input_back.reshape(devices * CAP, model_width),
        contract_first,
        preferred_element_type=jnp.float32,
    ).astype(jnp.bfloat16)
    token_back = jnp.sum(
        dispatch_mat.astype(jnp.float32) * weights_back.reshape(-1).astype(jnp.float32)[:, None],
        axis=0,
    )
    route_grad = jnp.where(live_slot, token_back[:, None], 0.0).astype(jnp.bfloat16)
    return (
        query_grad,
        key_grad,
        value_grad,
        gate_grad,
        input_grad,
        route_grad,
        gate_proj_grad,
        up_proj_grad,
        down_proj_grad,
    )


def solution(mesh):
    return jax.shard_map(
        shards,
        mesh=mesh,
        in_specs=(
            P("dp", "expert", None),
            P("dp", "expert", None),
            P("dp", "expert", None),
            P("dp", "expert", None),
            P("dp", "expert", None),
            P(("dp", "expert"), None),
            P(("dp", "expert"), None),
            P(("dp", "expert"), None),
            P(("dp", "expert"), None),
            P("expert", "dp", None),
            P("expert", "dp", None),
            P("expert", None, "dp"),
        ),
        out_specs=(
            P("dp", "expert", None),
            P("dp", "expert", None),
            P("dp", "expert", None),
            P("dp", "expert", None),
            P(("dp", "expert"), None),
            P(("dp", "expert"), None),
            P("expert", "dp", None),
            P("expert", "dp", None),
            P("expert", None, "dp"),
        ),
        check_vma=False,
    )
```
